32 devices in a mesh: cand: 4 (over x, core), seq: 8 (over z, y).
Axes of the slice: x: 2, y: 2, z: 4, core: 2. Of those that a mesh axis runs over, the one named last changes fastest.
Arguments:
- response_query_array: bfloat16 [8, 768, 2560], P('cand', 'seq'), may hold values from -180 to 180
- response_key_array: bfloat16 [8, 768, 512], P('cand', 'seq'), may hold values from -6 to 6
- response_value_array: bfloat16 [8, 768, 512], P('cand', 'seq'), may hold values from -6 to 6
- prompt_key_array: bfloat16 [2048, 512], P(('cand', 'seq')), may hold values from -6 to 6
- prompt_value_array: bfloat16 [2048, 512], P(('cand', 'seq')), may hold values from -6 to 6
- lengths: int32 [8], replicated, may hold values from 192 to 768, as said below
- offsets: int32 [8], replicated, may hold values from 512 to 2048, as said below
- ranks: int32 [8], replicated, may hold values from 0 to 7, each once
Outputs:
- attention: bfloat16 [8, 768, 2560], P('cand', 'seq')
The draws below stay inside these ranges and needn't reach their ends.
Inputs may be any that keep to these rules, and one draw needn't show every extreme that they name: `lengths`: some candidate's response has all 768 positions live. `offsets`: some candidate sees the whole prompt.
All inputs are finite; a program needn't handle non-finite values.
Results may differ from the reference program's by a relative error of at most 0.004.
Values may be sent and summed in bfloat16 or wider, within the bound.
No kernel may reach another device: no remote copies, remote signals or barrier semaphores. Data moves between devices by JAX's collectives and lax.ppermute only.
A program may use at most 128 MiB of HBM per device.

```python
import math
import jax
import jax.numpy as jnp
from jax import lax

QUERY_HEADS = 20
KEY_VALUE_HEADS = 4
HEAD_DIMENSION = 128
CANDIDATE_COUNT = 8
RESPONSE_LENGTH = 768
PROMPT_LENGTH = 2048


def prompt_keys_base(key):
    base_offset = jax.random.normal(jax.random.fold_in(key, 7), (PROMPT_LENGTH, KEY_VALUE_HEADS * HEAD_DIMENSION), jnp.float32)
    base_offset = jnp.clip(base_offset, -6.0, 6.0)
    return base_offset


def draw_prompt_key_array(key, part):
    return prompt_keys_base(key).astype(jnp.bfloat16)


def draw_response_query_array(key, part):
    values = 2.5 * jnp.clip(jax.random.normal(jax.random.fold_in(key, 11), (CANDIDATE_COUNT, RESPONSE_LENGTH, QUERY_HEADS * HEAD_DIMENSION), jnp.float32), -6.0, 6.0)
    return values.astype(jnp.bfloat16)


def draw_lengths(key, part):
    raw = jax.random.randint(jax.random.fold_in(key, 21), (CANDIDATE_COUNT,), RESPONSE_LENGTH // 4, RESPONSE_LENGTH + 1)
    longest = jax.random.randint(jax.random.fold_in(key, 22), (), 0, CANDIDATE_COUNT)
    return jnp.where(jnp.arange(CANDIDATE_COUNT) == longest, RESPONSE_LENGTH, raw).astype(jnp.int32)


def draw_offsets(key, part):
    raw = jax.random.randint(jax.random.fold_in(key, 31), (CANDIDATE_COUNT,), PROMPT_LENGTH // 4, PROMPT_LENGTH + 1)
    widest = jax.random.randint(jax.random.fold_in(key, 32), (), 0, CANDIDATE_COUNT)
    return jnp.where(jnp.arange(CANDIDATE_COUNT) == widest, PROMPT_LENGTH, raw).astype(jnp.int32)


def block_levels(stream_key, shape, cuts, least, top_value):
    def one(position, shards_of):
        heights = jax.random.uniform(jax.random.fold_in(jax.random.fold_in(stream_key, 6), position), (shards_of,), jnp.float32, least / len(cuts), top_value / len(cuts))
        return jnp.repeat(jnp.exp(heights), shape[position] // shards_of).reshape((-1,) + (1,) * (len(shape) - position - 1))

    loudness = one(*cuts[0])
    for cut in cuts[1:]:
        loudness = loudness * one(*cut)
    return loudness


def gaussian(own_key, shape, width, limit, cuts=(), kind=jnp.bfloat16):
    factor_of = block_levels(own_key, shape, cuts, -0.22, 0.18) if cuts else 1.0
    drawn = jax.random.normal(own_key, shape, jnp.float32) * width * factor_of
    return jnp.minimum(jnp.maximum(drawn, -limit), limit).astype(kind)


def setup_inputs(seed: int = 0) -> dict:
    streams_of = jax.random.split(jax.random.key(seed), 9)
    return {
        "response_query_array": draw_response_query_array(jax.random.fold_in(streams_of[8], 71), 0),
        "response_key_array": gaussian(streams_of[1], (CANDIDATE_COUNT, RESPONSE_LENGTH, KEY_VALUE_HEADS * HEAD_DIMENSION), 1.0, 6.0, ((0, 4), (1, 8))),
        "response_value_array": gaussian(streams_of[2], (CANDIDATE_COUNT, RESPONSE_LENGTH, KEY_VALUE_HEADS * HEAD_DIMENSION), 1.0, 6.0, ((0, 4), (1, 8))),
        "prompt_key_array": draw_prompt_key_array(jax.random.fold_in(streams_of[8], 71), 0),
        "prompt_value_array": gaussian(streams_of[4], (PROMPT_LENGTH, KEY_VALUE_HEADS * HEAD_DIMENSION), 1.0, 6.0, ((0, 32),)),
        "lengths": draw_lengths(jax.random.fold_in(streams_of[8], 71), 0),
        "offsets": draw_offsets(jax.random.fold_in(streams_of[8], 71), 0),
        "ranks": jax.random.permutation(streams_of[7], CANDIDATE_COUNT).astype(jnp.int32),
    }


def candidate_attention(single_query, single_key, single_value, prompt_key_array, prompt_value_array, length, offset):
    group_width = QUERY_HEADS // KEY_VALUE_HEADS
    score_scale = 1.0 / math.sqrt(HEAD_DIMENSION)
    query_rows = single_query.astype(jnp.float32).reshape(RESPONSE_LENGTH, KEY_VALUE_HEADS, group_width, HEAD_DIMENSION).transpose(1, 2, 0, 3)
    prompt_key_rows = prompt_key_array.astype(jnp.float32).reshape(PROMPT_LENGTH, KEY_VALUE_HEADS, HEAD_DIMENSION).transpose(1, 0, 2)
    prompt_value_rows = prompt_value_array.astype(jnp.float32).reshape(PROMPT_LENGTH, KEY_VALUE_HEADS, HEAD_DIMENSION).transpose(1, 0, 2)
    response_key_rows = single_key.astype(jnp.float32).reshape(RESPONSE_LENGTH, KEY_VALUE_HEADS, HEAD_DIMENSION).transpose(1, 0, 2)
    response_value_rows = single_value.astype(jnp.float32).reshape(RESPONSE_LENGTH, KEY_VALUE_HEADS, HEAD_DIMENSION).transpose(1, 0, 2)
    prompt_pos = jnp.arange(PROMPT_LENGTH, dtype=jnp.int32)
    resp_pos = jnp.arange(RESPONSE_LENGTH, dtype=jnp.int32)
    prompt_allowed = (prompt_pos < offset)[None, None, :]
    resp_allowed = ((resp_pos[None, :] <= resp_pos[:, None]) & (resp_pos[None, :] < length))[None]

    def one_head(pieces):
        head_query, head_pkeys, head_pvalues, head_rkeys, head_rvalues = pieces
        prompt_scores = jnp.einsum('grd,nd->grn', head_query, head_pkeys) * score_scale
        prompt_scores = jnp.where(prompt_allowed, prompt_scores, -jnp.inf)
        resp_scores = jnp.einsum('grd,nd->grn', head_query, head_rkeys) * score_scale
        resp_scores = jnp.where(resp_allowed, resp_scores, -jnp.inf)
        top_score = jnp.maximum(lax.optimization_barrier(jnp.max(prompt_scores, axis=-1)), lax.optimization_barrier(jnp.max(resp_scores, axis=-1)))
        prompt_exp = jnp.exp(prompt_scores - top_score[..., None])
        resp_exp = jnp.exp(resp_scores - top_score[..., None])
        denominator = lax.optimization_barrier(jnp.sum(prompt_exp, axis=-1)) + lax.optimization_barrier(jnp.sum(resp_exp, axis=-1))
        prompt_weights = lax.optimization_barrier(prompt_exp.astype(jnp.bfloat16)).astype(jnp.float32)
        resp_weights = lax.optimization_barrier(resp_exp.astype(jnp.bfloat16)).astype(jnp.float32)
        summed = jnp.einsum('grn,nd->grd', prompt_weights, head_pvalues)
        summed = summed + jnp.einsum('grn,nd->grd', resp_weights, head_rvalues)
        return summed / denominator[..., None]
    attended = lax.map(one_head, (query_rows, prompt_key_rows, prompt_value_rows, response_key_rows, response_value_rows))
    attended = attended.transpose(2, 0, 1, 3).reshape(RESPONSE_LENGTH, QUERY_HEADS * HEAD_DIMENSION)
    row_valid = (resp_pos < length)[:, None]
    return jnp.where(row_valid, attended, 0.0).astype(jnp.bfloat16)

def reference(response_query_array, response_key_array, response_value_array, prompt_key_array, prompt_value_array, lengths, offsets, ranks):

    def per_candidate(pieces):
        single_query, single_key, single_value, length, offset = pieces
        return candidate_attention(single_query, single_key, single_value, prompt_key_array, prompt_value_array, length, offset)
    attended = lax.map(per_candidate, (response_query_array, response_key_array, response_value_array, lengths, offsets))
    every_cand = jnp.arange(CANDIDATE_COUNT, dtype=jnp.int32)
    matches = ranks[None, :] == every_cand[:, None]
    source = lax.optimization_barrier(jnp.sum(jnp.where(matches, every_cand[None, :], 0), axis=1)).astype(jnp.int32)
    return jnp.take(attended, source, axis=0)
```

```python
import functools
import math

import jax
import jax.numpy as jnp
from jax import lax
from jax.experimental import pallas as pl
from jax.experimental.pallas import tpu as pltpu
from jax.sharding import PartitionSpec as P

QUERY_HEADS = 20
KEY_VALUE_HEADS = 4
HEAD_DIMENSION = 128
GROUP = QUERY_HEADS // KEY_VALUE_HEADS
SCORE_FACTOR = math.log2(math.e) / math.sqrt(HEAD_DIMENSION)
LOWEST = -1e30
AXES = ("cand", "seq")
VMEM_LIMIT = 56 * 1024 * 1024


class Layout:
    def __init__(self, cand_count, seq_count):
        self.cand_count = cand_count
        self.seq_count = seq_count
        self.cores = 2 if cand_count % 2 == 0 else 1
        self.outers = cand_count // self.cores
        self.zs = math.gcd(seq_count, 4)
        self.inners = seq_count // self.zs

    def permute(self, array, outer=0, core=0, z=0, inner=0):
        pairs = []
        for o in range(self.outers):
            for c in range(self.cores):
                for k in range(self.zs):
                    for i in range(self.inners):
                        source = ((o * self.cores + c) * self.zs + k) * self.inners + i
                        o2, c2 = (o + outer) % self.outers, (c + core) % self.cores
                        k2, i2 = (k + z) % self.zs, (i + inner) % self.inners
                        target = ((o2 * self.cores + c2) * self.zs + k2) * self.inners + i2
                        pairs.append((source, target))
        return lax.ppermute(array, AXES, pairs)


def online_step(q, k, v, mask, m_ref, l_ref, acc_ref):
    scores = lax.dot_general(q, k, (((1,), (1,)), ((), ())), preferred_element_type=jnp.float32)
    scores = scores * SCORE_FACTOR
    if mask is not None:
        scores = jnp.where(mask, scores, LOWEST)
    m_old = m_ref[...]
    m_new = jnp.maximum(m_old, jnp.max(scores, axis=1, keepdims=True))
    scale = jnp.exp2(m_old - m_new)
    weights = jnp.exp2(scores - m_new[:, :1])
    l_ref[...] = l_ref[...] * scale + jnp.sum(weights, axis=1, keepdims=True)
    acc_ref[...] = acc_ref[...] * scale + jnp.dot(
        weights.astype(jnp.bfloat16), v, preferred_element_type=jnp.float32
    )
    m_ref[...] = m_new


def load_queries(q_ref, a, h):
    base = h * GROUP * HEAD_DIMENSION
    parts = [
        q_ref[a, :, base + g * HEAD_DIMENSION : base + (g + 1) * HEAD_DIMENSION]
        for g in range(GROUP)
    ]
    return jnp.concatenate(parts, axis=0)


def prompt_kernel(layout, heads, chunk, info_ref, q_ref, *refs):
    piece_count = layout.outers * layout.cores
    pieces = refs[:piece_count]
    acc_ref, m_ref, l_ref = refs[piece_count : piece_count + 3]
    k_all, v_all = refs[piece_count + 3 :]
    rows = pieces[0].shape[0] // (layout.zs * layout.inners)
    outer, core, z, inner = info_ref[0], info_ref[1], info_ref[2], info_ref[3]
    cands = q_ref.shape[0]
    for h in range(heads):
        for o in range(layout.outers):
            for c in range(layout.cores):
                piece = pieces[o * layout.cores + c]
                o_from = lax.rem(outer + layout.outers - o, layout.outers)
                c_from = lax.rem(core + layout.cores - c, layout.cores)
                for i in range(layout.inners):
                    for k in range(layout.zs):
                        i_from = lax.rem(inner + layout.inners - i, layout.inners)
                        z_from = lax.rem(z + layout.zs - k, layout.zs)
                        at = ((o_from * layout.cores + c_from) * layout.zs + z_from) * layout.inners
                        at = pl.multiple_of((at + i_from) * rows, rows)
                        here = (i * layout.zs + k) * rows
                        lanes = slice(h * HEAD_DIMENSION, (h + 1) * HEAD_DIMENSION)
                        k_all[pl.ds(at, rows), :] = piece[here : here + rows, lanes]
                        lanes = slice(
                            (heads + h) * HEAD_DIMENSION, (heads + h + 1) * HEAD_DIMENSION
                        )
                        v_all[pl.ds(at, rows), :] = piece[here : here + rows, lanes]
        for a in range(cands):
            length, offset = info_ref[4 + a], info_ref[4 + cands + a]
            m_at, l_at, acc_at = m_ref.at[a, h], l_ref.at[a, h], acc_ref.at[a, h]
            m_at[...] = jnp.full(m_at.shape, LOWEST, jnp.float32)
            l_at[...] = jnp.zeros(l_at.shape, jnp.float32)
            acc_at[...] = jnp.zeros(acc_at.shape, jnp.float32)
            first = (z * layout.inners + inner) * q_ref.shape[1]

            @pl.when(first < length)
            def _():
                q = load_queries(q_ref, a, h)

                def full(step, carry):
                    at = pl.multiple_of(step * chunk, chunk)
                    online_step(
                        q, k_all[pl.ds(at, chunk), :], v_all[pl.ds(at, chunk), :], None,
                        m_at, l_at, acc_at,
                    )
                    return carry

                whole = offset // chunk
                lax.fori_loop(0, whole, full, 0)

                @pl.when(whole * chunk < offset)
                def _():
                    at = pl.multiple_of(whole * chunk, chunk)
                    place = lax.broadcasted_iota(jnp.int32, (q.shape[0], chunk), 1) + at
                    online_step(
                        q, k_all[pl.ds(at, chunk), :], v_all[pl.ds(at, chunk), :],
                        place < offset, m_at, l_at, acc_at,
                    )


def response_kernel(layout, heads, chunk, info_ref, q_ref, acc_ref, m_ref, l_ref, *refs):
    piece_count = layout.zs * layout.inners
    pieces = refs[:piece_count]
    out_ref = refs[piece_count]
    k_all, v_all, m_at, l_at, acc_at = refs[piece_count + 1 :]
    z, inner = info_ref[2], info_ref[3]
    cands, rows = q_ref.shape[0], q_ref.shape[1]
    first = (z * layout.inners + inner) * rows
    for a in range(cands):
        length = info_ref[4 + a]

        @pl.when(first >= length)
        def _():
            out_ref[a] = jnp.zeros(out_ref.shape[1:], out_ref.dtype)

        @pl.when(first < length)
        def _():
            for h in range(heads):
                for k in range(layout.zs):
                    for i in range(layout.inners):
                        z_from = lax.rem(z + layout.zs - k, layout.zs)
                        i_from = lax.rem(inner + layout.inners - i, layout.inners)
                        at = pl.multiple_of((z_from * layout.inners + i_from) * rows, rows)
                        piece = pieces[k * layout.inners + i]
                        lanes = slice(h * HEAD_DIMENSION, (h + 1) * HEAD_DIMENSION)
                        k_all[pl.ds(at, rows), :] = piece[a, :, lanes]
                        lanes = slice(
                            (heads + h) * HEAD_DIMENSION, (heads + h + 1) * HEAD_DIMENSION
                        )
                        v_all[pl.ds(at, rows), :] = piece[a, :, lanes]
                m_at[...] = m_ref[a, h]
                l_at[...] = l_ref[a, h]
                acc_at[...] = acc_ref[a, h]
                q = load_queries(q_ref, a, h)
                row = lax.broadcasted_iota(jnp.int32, (rows, chunk), 0) + first
                row = jnp.concatenate([row] * GROUP, axis=0)
                column = lax.broadcasted_iota(jnp.int32, (GROUP * rows, chunk), 1)

                def step(n, carry):
                    at = pl.multiple_of(n * chunk, chunk)
                    place = column + at
                    mask = (place <= row) & (place < length)
                    online_step(
                        q, k_all[pl.ds(at, chunk), :], v_all[pl.ds(at, chunk), :], mask,
                        m_at, l_at, acc_at,
                    )
                    return carry

                last = jnp.minimum(first + rows, length)
                lax.fori_loop(0, (last + chunk - 1) // chunk, step, 0)
                mixed = acc_at[...] / l_at[...]
                live = lax.broadcasted_iota(jnp.int32, (rows, HEAD_DIMENSION), 0) + first < length
                for g in range(GROUP):
                    lane = (h * GROUP + g) * HEAD_DIMENSION
                    part = jnp.where(live, mixed[g * rows : (g + 1) * rows], 0.0)
                    out_ref[a, :, lane : lane + HEAD_DIMENSION] = part.astype(jnp.bfloat16)


def divisor(total, *choices):
    for choice in choices:
        if total % choice == 0:
            return choice
    return total


def run_prompt(layout, heads, info, q, pieces):
    cands, rows = q.shape[0], q.shape[1]
    keys = pieces[0].shape[0] * len(pieces)
    state = (cands, heads, GROUP * rows, HEAD_DIMENSION)
    flops = 4 * cands * heads * GROUP * rows * keys * HEAD_DIMENSION
    return pl.pallas_call(
        functools.partial(prompt_kernel, layout, heads, divisor(keys, 512, 256, 128)),
        out_shape=[jax.ShapeDtypeStruct(state, jnp.float32)] * 3,
        in_specs=[pl.BlockSpec(memory_space=pltpu.SMEM)]
        + [pl.BlockSpec(memory_space=pltpu.VMEM)] * (1 + len(pieces)),
        out_specs=[pl.BlockSpec(memory_space=pltpu.VMEM)] * 3,
        scratch_shapes=[pltpu.VMEM((keys, HEAD_DIMENSION), jnp.bfloat16)] * 2,
        compiler_params=pltpu.CompilerParams(vmem_limit_bytes=VMEM_LIMIT),
        cost_estimate=pl.CostEstimate(
            flops=flops, transcendentals=flops // 512, bytes_accessed=4 * keys * 256 * heads
        ),
        name="prompt_part",
    )(info, q, *pieces)


def run_response(layout, heads, info, q, state, pieces):
    cands, rows = q.shape[0], q.shape[1]
    keys = rows * len(pieces)
    flops = 4 * cands * heads * GROUP * rows * keys * HEAD_DIMENSION
    return pl.pallas_call(
        functools.partial(response_kernel, layout, heads, divisor(keys, 256, 192, 128)),
        out_shape=jax.ShapeDtypeStruct(q.shape, jnp.bfloat16),
        in_specs=[pl.BlockSpec(memory_space=pltpu.SMEM)]
        + [pl.BlockSpec(memory_space=pltpu.VMEM)] * (4 + len(pieces)),
        out_specs=pl.BlockSpec(memory_space=pltpu.VMEM),
        scratch_shapes=[pltpu.VMEM((keys, HEAD_DIMENSION), jnp.bfloat16)] * 2
        + [pltpu.VMEM((GROUP * rows, HEAD_DIMENSION), jnp.float32)] * 3,
        compiler_params=pltpu.CompilerParams(vmem_limit_bytes=VMEM_LIMIT),
        cost_estimate=pl.CostEstimate(
            flops=flops, transcendentals=flops // 512, bytes_accessed=4 * keys * 256 * heads
        ),
        name="response_part",
    )(info, q, *state, *pieces)


def gather_prompt(layout, block):
    ring = [block]
    for _ in range(layout.zs - 1):
        ring.append(layout.permute(ring[-1], z=1))
    column = jnp.concatenate(ring, axis=0)
    around = [column] + [layout.permute(column, inner=i) for i in range(1, layout.inners)]
    plane = jnp.concatenate(around, axis=0)
    pieces = []
    for o in range(layout.outers):
        across = layout.permute(plane, outer=o) if o else plane
        pieces.append(across)
        for c in range(1, layout.cores):
            pieces.append(layout.permute(across, core=c))
    return pieces


def gather_response(layout, block):
    pieces = []
    for k in range(layout.zs):
        if k:
            block = layout.permute(block, z=1)
        pieces.append(block)
        for i in range(1, layout.inners):
            pieces.append(layout.permute(block, inner=i))
    return pieces


def place_by_rank(layout, attended, ranks, group_at):
    count = attended.shape[0]
    every = jnp.arange(ranks.shape[0], dtype=jnp.int32)
    core_at = group_at % layout.cores
    outer_at = group_at // layout.cores

    def source_of(rank):
        return jnp.sum(jnp.where(ranks == rank, every, 0))

    held = [attended] + [layout.permute(attended, outer=o) for o in range(1, layout.outers)]
    held = jnp.concatenate(held, axis=0)

    def slot_of(source):
        o_from = source // count // layout.cores
        return lax.rem(outer_at + layout.outers - o_from, layout.outers) * count + source % count

    def pick(rank):
        return lax.dynamic_index_in_dim(held, slot_of(source_of(rank)), 0, keepdims=False)

    chosen = [pick(group_at * count + within) for within in range(count)]
    for c in range(1, layout.cores):
        other = outer_at * layout.cores + lax.rem(core_at + c, layout.cores)
        sent = jnp.stack([pick(other * count + within) for within in range(count)])
        arrived = layout.permute(sent, core=c)
        owner = lax.rem(core_at + layout.cores - c, layout.cores)
        for within in range(count):
            from_core = source_of(group_at * count + within) // count % layout.cores
            chosen[within] = jnp.where(from_core == owner, arrived[within], chosen[within])
    return jnp.stack(chosen)


def body(layout, q, rk, rv, pk, pv, lengths, offsets, ranks):
    cands, rows = q.shape[0], q.shape[1]
    group_at = lax.axis_index("cand")
    seq_at = lax.axis_index("seq")
    mine = group_at * cands
    info = jnp.concatenate(
        [
            jnp.stack(
                [
                    group_at // layout.cores,
                    group_at % layout.cores,
                    seq_at // layout.inners,
                    seq_at % layout.inners,
                ]
            ).astype(jnp.int32),
            lax.dynamic_slice_in_dim(lengths, mine, cands),
            lax.dynamic_slice_in_dim(offsets, mine, cands),
        ]
    )
    groups = [(0, KEY_VALUE_HEADS)]
    finished = []
    for low, high in groups:
        heads = high - low
        lanes = slice(low * HEAD_DIMENSION, high * HEAD_DIMENSION)
        q_part = q[:, :, low * GROUP * HEAD_DIMENSION : high * GROUP * HEAD_DIMENSION]
        prompt = gather_prompt(layout, jnp.concatenate([pk[:, lanes], pv[:, lanes]], axis=1))
        response = gather_response(
            layout, jnp.concatenate([rk[:, :, lanes], rv[:, :, lanes]], axis=2)
        )
        state = run_prompt(layout, heads, info, q_part, prompt)
        mixed = run_response(layout, heads, info, q_part, state, response)
        finished.append(place_by_rank(layout, mixed, ranks, group_at))
    return jnp.concatenate(finished, axis=2)


def solution(mesh):
    layout = Layout(mesh.shape["cand"], mesh.shape["seq"])
    in_specs = (
        P("cand", "seq", None),
        P("cand", "seq", None),
        P("cand", "seq", None),
        P(("cand", "seq"), None),
        P(("cand", "seq"), None),
        P(),
        P(),
        P(),
    )
    out_specs = P("cand", "seq", None)
    return jax.shard_map(
        functools.partial(body, layout),
        mesh=mesh,
        in_specs=in_specs,
        out_specs=out_specs,
        check_vma=False,
    )
```

```python
import functools
import math

import jax
import jax.numpy as jnp
from jax import lax
from jax.experimental import pallas as pl
from jax.experimental.pallas import tpu as pltpu
from jax.sharding import PartitionSpec as P

QUERY_HEADS = 20
KEY_VALUE_HEADS = 4
HEAD = 128
GROUP = QUERY_HEADS // KEY_VALUE_HEADS
WIDE = GROUP * HEAD
SCORE_FACTOR = math.log2(math.e) / math.sqrt(HEAD)
LOWEST = -1e30
AXES = ("cand", "seq")
VMEM_LIMIT = 56 * 1024 * 1024
VMEM = pl.BlockSpec(memory_space=pltpu.VMEM)
SMEM = pl.BlockSpec(memory_space=pltpu.SMEM)

FIELDS = 5


class Layout:
    def __init__(self, mesh):
        assert mesh.shape["cand"] == 4 and mesh.shape["seq"] % 2 == 0
        self.rings = mesh.shape["seq"] // 2

    def permute(self, array, d=0, core=0, ring=0):
        pairs = []
        for x in range(2):
            for c in range(2):
                for r in range(self.rings):
                    for y in range(2):
                        source = ((x * 2 + c) * self.rings + r) * 2 + y
                        target = ((x ^ (d >> 1)) * 2 + (c ^ core)) * self.rings
                        target = (target + (r + ring) % self.rings) * 2 + (y ^ (d & 1))
                        pairs.append((source, target))
        return lax.ppermute(array, AXES, pairs)

    def exchange(self, pieces):
        return [pieces[0]] + [self.permute(pieces[d], d=d) for d in range(1, 4)]

    def ring_gather(self, block):
        pieces = [block]
        for _ in range(self.rings - 1):
            pieces.append(self.permute(pieces[-1], ring=1))
        return pieces


def kernel_call(kernel, out_shape, operands, scratch=(), cost=(0, 0), name=None):
    many = isinstance(out_shape, list)
    return pl.pallas_call(
        kernel,
        out_shape=out_shape,
        in_specs=[SMEM] + [VMEM] * (len(operands) - 1),
        out_specs=[VMEM] * len(out_shape) if many else VMEM,
        scratch_shapes=list(scratch),
        compiler_params=pltpu.CompilerParams(vmem_limit_bytes=VMEM_LIMIT),
        cost_estimate=pl.CostEstimate(
            flops=cost[0], transcendentals=cost[0] // 512, bytes_accessed=cost[1]
        ),
        name=name,
    )(*operands)


def pack_keys_kernel(info, rk, rv, pk, pv, *outs):
    cands, rows = rk.shape[0], rk.shape[1]
    own = info[0] * 2 + info[3]
    for d, out in enumerate(outs):
        lane = pl.ds(pl.multiple_of((own ^ d) * HEAD, HEAD), HEAD)
        for w in range(cands):
            out[w * rows : (w + 1) * rows, :HEAD] = rk[w, :, lane]
            out[w * rows : (w + 1) * rows, HEAD:] = rv[w, :, lane]
        out[cands * rows :, :HEAD] = pk[:, lane]
        out[cands * rows :, HEAD:] = pv[:, lane]


def pack_queries_kernel(info, q, *outs):
    own = info[0] * 2 + info[3]
    for d, out in enumerate(outs):
        lane = pl.ds(pl.multiple_of((own ^ d) * WIDE, HEAD), WIDE)
        for w in range(q.shape[0]):
            out[w] = q[w, :, lane]


def unit_info(info, unit, field):
    return info[4 + unit * FIELDS + field]


def select_keys_kernel(cands, rows, info, own, other, *outs):
    for w, out in enumerate(outs):
        for dx in range(2):
            unit = w * 2 + dx
            away = unit_info(info, unit, 0)
            home = unit_info(info, unit, 1)
            row = pl.ds(pl.multiple_of(unit_info(info, unit, 2) * rows, rows), rows)
            for dy in range(2):
                d = home * 2 + dy
                out[dx, dy] = jnp.where(away == 1, other[d, row, :], own[d, row, :])


def load_queries(info, unit, q_own, q_other, q_all):
    rows = q_own.shape[2]
    away, home, slot = (unit_info(info, unit, n) for n in range(3))
    for dy in range(2):
        d = home * 2 + dy
        block = jnp.where(away == 1, q_other[d, slot], q_own[d, slot])
        for g in range(GROUP):
            at = (g * 2 + dy) * rows
            q_all[at : at + rows, :] = block[:, g * HEAD : (g + 1) * HEAD]


def online_step(q, k, v, mask, state):
    top, total, mixed = state
    scores = lax.dot_general(k, q, (((1,), (1,)), ((), ())), preferred_element_type=jnp.float32)
    scores = scores * SCORE_FACTOR
    if mask is not None:
        scores = jnp.where(mask, scores, LOWEST)
    new_top = jnp.maximum(top, jnp.max(scores, axis=0, keepdims=True))
    scale = jnp.exp2(top - new_top)
    weights = jnp.exp2(scores - new_top)
    total = total * scale + jnp.sum(weights, axis=0, keepdims=True)
    mixed = mixed * scale + lax.dot_general(
        v, weights.astype(jnp.bfloat16), (((0,), (0,)), ((), ())),
        preferred_element_type=jnp.float32,
    )
    return new_top, total, mixed


def prompt_kernel(layout, slots, chunk, info, q_own, q_other, p_own, p_other, *refs):
    mixed_ref, top_ref, total_ref, k_all, v_all, q_all = refs
    x, core, r, y = info[0], info[1], info[2], info[3]
    rows = p_own.shape[0] // (layout.rings * 4)
    queries = q_all.shape[0]
    for o, piece in enumerate((p_own, p_other)):
        for k in range(layout.rings):
            for d in range(4):
                group = (x ^ (d >> 1)) * 2 + (core ^ o)
                seq = lax.rem(r + layout.rings - k, layout.rings) * 2 + (y ^ (d & 1))
                at = pl.multiple_of((group * layout.rings * 2 + seq) * rows, rows)
                here = (k * 4 + d) * rows
                k_all[pl.ds(at, rows), :] = piece[here : here + rows, :HEAD]
                v_all[pl.ds(at, rows), :] = piece[here : here + rows, HEAD:]
    for n, unit in enumerate(slots):
        length, offset = unit_info(info, unit, 3), unit_info(info, unit, 4)

        @pl.when(r * (queries // GROUP) < length)
        def _():
            load_queries(info, unit, q_own, q_other, q_all)

            def run(step, state, masked):
                at = pl.multiple_of(step * chunk, chunk)
                mask = None
                if masked:
                    place = lax.broadcasted_iota(jnp.int32, (chunk, queries), 0) + at
                    mask = place < offset
                return online_step(
                    q_all[...], k_all[pl.ds(at, chunk), :], v_all[pl.ds(at, chunk), :], mask, state
                )

            state = (
                jnp.full((1, queries), LOWEST, jnp.float32),
                jnp.zeros((1, queries), jnp.float32),
                jnp.zeros((HEAD, queries), jnp.float32),
            )
            whole = offset // chunk
            state = lax.fori_loop(0, whole, lambda i, s: run(i, s, False), state)
            top_ref[n], total_ref[n], mixed_ref[n] = state

            @pl.when(whole * chunk < offset)
            def _():
                state = run(whole, (top_ref[n], total_ref[n], mixed_ref[n]), True)
                top_ref[n], total_ref[n], mixed_ref[n] = state


def response_kernel(layout, w, chunk, info, place_ref, q_own, q_other, mixed, top, total, *refs):
    pieces, outs = refs[: layout.rings], refs[layout.rings : layout.rings + 4]
    k_all, v_all, q_all = refs[layout.rings + 4 :]
    r, y = info[2], info[3]
    rows = outs[0].shape[0]
    queries = q_all.shape[0]
    for dx in range(2):
        unit = w * 2 + dx
        length = unit_info(info, unit, 3)

        @pl.when(r * (2 * rows) >= length)
        def _():
            for dy in range(2):
                outs[dx * 2 + dy][...] = jnp.zeros((rows, WIDE), jnp.bfloat16)

        @pl.when(r * (2 * rows) < length)
        def _():
            load_queries(info, unit, q_own, q_other, q_all)
            for k, piece in enumerate(pieces):
                for dy in range(2):
                    seq = lax.rem(r + layout.rings - k, layout.rings) * 2 + (y ^ dy)
                    at = pl.multiple_of(seq * rows, rows)
                    k_all[pl.ds(at, rows), :] = piece[dx, dy, :, :HEAD]
                    v_all[pl.ds(at, rows), :] = piece[dx, dy, :, HEAD:]
            place = place_ref[...]

            def run(step, state):
                at = pl.multiple_of(step * chunk, chunk)
                key = lax.broadcasted_iota(jnp.int32, (chunk, queries), 0) + at
                mask = key <= jnp.minimum(place, length - 1)
                return online_step(
                    q_all[...], k_all[pl.ds(at, chunk), :], v_all[pl.ds(at, chunk), :], mask, state
                )

            last = jnp.minimum((r + 1) * 2 * rows, length)
            state = (top[dx], total[dx], mixed[dx])
            _, sums, out = lax.fori_loop(0, (last + chunk - 1) // chunk, run, state)
            out = jnp.where(place < length, out / sums, 0.0).T
            for dy in range(2):
                for g in range(GROUP):
                    at = (g * 2 + dy) * rows
                    part = out[at : at + rows].astype(jnp.bfloat16)
                    outs[dx * 2 + dy][:, g * HEAD : (g + 1) * HEAD] = part


def join_kernel(info, *refs):
    pieces, out = refs[:-1], refs[-1]
    own = info[0] * 2 + info[3]
    for w in range(out.shape[0]):
        for d in range(4):
            lane = pl.ds(pl.multiple_of((own ^ d) * WIDE, HEAD), WIDE)
            out[w, :, lane] = pieces[w * 4 + d][...]


def divisor(total, *choices):
    for choice in choices:
        if total % choice == 0:
            return choice
    return total


def struct(*shape, dtype=jnp.bfloat16):
    return jax.ShapeDtypeStruct(shape, dtype)


def device_info(cands, lengths, offsets, ranks):
    group = lax.axis_index("cand").astype(jnp.int32)
    seq = lax.axis_index("seq").astype(jnp.int32)
    x, core = group // 2, group % 2
    every = jnp.arange(ranks.shape[0], dtype=jnp.int32)
    values = [x, core, seq // 2, seq % 2]
    for w in range(cands):
        for dx in range(2):
            rank = ((x ^ dx) * 2 + core) * cands + w
            hit = (ranks == rank).astype(jnp.int32)
            source = jnp.sum(hit * every)
            home = source // cands
            values += [
                (home % 2) ^ core,
                (home // 2) ^ x,
                source % cands,
                jnp.sum(hit * lengths),
                jnp.sum(hit * offsets),
            ]
    return jnp.stack(values)


def body(layout, q, rk, rv, pk, pv, lengths, offsets, ranks):
    cands, rows = q.shape[0], q.shape[1]
    prompt_rows = pk.shape[0]
    queries = 2 * rows * GROUP
    info = device_info(cands, lengths, offsets, ranks)
    bf16 = functools.partial(pltpu.VMEM, dtype=jnp.bfloat16)

    packed = struct(cands * rows + prompt_rows, 2 * HEAD)
    keys = kernel_call(
        pack_keys_kernel, [packed] * 4, (info, rk, rv, pk, pv), name="pack_keys"
    )
    asked = kernel_call(
        pack_queries_kernel, [struct(cands, rows, WIDE)] * 4, (info, q), name="pack_queries"
    )
    keys = jnp.stack(layout.exchange(keys))
    prompt = keys[:, cands * rows :, :].reshape(4 * prompt_rows, 2 * HEAD)
    prompt = jnp.concatenate(layout.ring_gather(prompt), axis=0)
    prompt_other = layout.permute(prompt, core=1)

    keys_other = layout.permute(keys, core=1)
    slots = kernel_call(
        functools.partial(select_keys_kernel, cands, rows),
        [struct(2, 2, rows, 2 * HEAD)] * cands,
        (info, keys, keys_other),
        name="select_keys",
    )
    asked = jnp.stack(layout.exchange(asked))
    asked_other = layout.permute(asked, core=1)
    base = jnp.arange(queries, dtype=jnp.int32)
    seq_of = info[2] * 2 + (info[3] ^ (base // rows % 2))
    place = (seq_of * rows + base % rows)[None, :]

    prompt_keys = 2 * prompt.shape[0]
    chunk = divisor(prompt_keys, 512, 256, 128)
    finished = []
    for w in range(cands):
        units = (w * 2, w * 2 + 1)
        state = kernel_call(
            functools.partial(prompt_kernel, layout, units, chunk),
            [
                struct(2, HEAD, queries, dtype=jnp.float32),
                struct(2, 1, queries, dtype=jnp.float32),
                struct(2, 1, queries, dtype=jnp.float32),
            ],
            (info, asked, asked_other, prompt, prompt_other),
            scratch=[bf16((prompt_keys, HEAD))] * 2 + [bf16((queries, HEAD))],
            cost=(8 * queries * prompt_keys * HEAD, 4 * prompt.size),
            name="prompt_part",
        )
        pieces = layout.ring_gather(slots[w])
        response_keys = layout.rings * 2 * rows
        outs = kernel_call(
            functools.partial(response_kernel, layout, w, divisor(response_keys, 384, 256, 128)),
            [struct(rows, WIDE)] * 4,
            (info, place, asked, asked_other, *state, *pieces),
            scratch=[bf16((response_keys, HEAD))] * 2 + [bf16((queries, HEAD))],
            cost=(8 * queries * response_keys * HEAD, 4 * slots[w].size * layout.rings),
            name="response_part",
        )
        finished += layout.exchange(outs)
    return kernel_call(
        join_kernel, struct(*q.shape), (info, *finished), name="join_heads"
    )


def solution(mesh):
    in_specs = (
        P("cand", "seq", None),
        P("cand", "seq", None),
        P("cand", "seq", None),
        P(("cand", "seq"), None),
        P(("cand", "seq"), None),
        P(),
        P(),
        P(),
    )
    return jax.shard_map(
        functools.partial(body, Layout(mesh)),
        mesh=mesh,
        in_specs=in_specs,
        out_specs=P("cand", "seq", None),
        check_vma=False,
    )
```

```python
import functools
import math

import jax
import jax.numpy as jnp
from jax import lax
from jax.experimental import pallas as pl
from jax.experimental.pallas import tpu as pltpu
from jax.sharding import PartitionSpec as P

QUERY_HEADS = 20
KEY_VALUE_HEADS = 4
HEAD = 128
GROUP = QUERY_HEADS // KEY_VALUE_HEADS
WIDE = GROUP * HEAD
SCORE_FACTOR = math.log2(math.e) / math.sqrt(HEAD)
LOWEST = -1e30
AXES = ("cand", "seq")
VMEM = pl.BlockSpec(memory_space=pltpu.VMEM)
SMEM = pl.BlockSpec(memory_space=pltpu.SMEM)

FIELDS = 5


class Layout:
    def __init__(self, mesh):
        assert mesh.shape["cand"] == 4 and mesh.shape["seq"] % 2 == 0
        self.rings = mesh.shape["seq"] // 2

    def permute(self, array, d=0, core=0, ring=0):
        pairs = []
        for x in range(2):
            for c in range(2):
                for r in range(self.rings):
                    for y in range(2):
                        source = ((x * 2 + c) * self.rings + r) * 2 + y
                        target = ((x ^ (d >> 1)) * 2 + (c ^ core)) * self.rings
                        target = (target + (r + ring) % self.rings) * 2 + (y ^ (d & 1))
                        pairs.append((source, target))
        return lax.ppermute(array, AXES, pairs)

    def exchange(self, pieces):
        return [pieces[0]] + [self.permute(pieces[d], d=d) for d in range(1, 4)]

    def ring_gather(self, block):
        return [block] + [self.permute(block, ring=k) for k in range(1, self.rings)]


def kernel_call(kernel, out_shape, operands, scratch=(), cost=(0, 0), name=None, scalars=1, spare=2 << 20):
    many = isinstance(out_shape, list)
    arrays = list(operands) + (list(out_shape) if many else [out_shape]) + list(scratch)
    held = sum(math.prod(a.shape) * jnp.dtype(a.dtype).itemsize for a in arrays)
    return pl.pallas_call(
        kernel,
        out_shape=out_shape,
        in_specs=[SMEM] * scalars + [VMEM] * (len(operands) - scalars),
        out_specs=[VMEM] * len(out_shape) if many else VMEM,
        scratch_shapes=list(scratch),
        compiler_params=pltpu.CompilerParams(vmem_limit_bytes=held + held // 4 + spare),
        cost_estimate=pl.CostEstimate(
            flops=cost[0], transcendentals=cost[0] // 512, bytes_accessed=cost[1]
        ),
        name=name,
    )(*operands)


def plan_kernel(cands, lengths, offsets, ranks, info):
    group, seq = lax.axis_index("cand"), lax.axis_index("seq")
    x, core = group // 2, group % 2
    info[0], info[1], info[2], info[3] = x, core, seq // 2, seq % 2
    for w in range(cands):
        for dx in range(2):
            rank = ((x ^ dx) * 2 + core) * cands + w
            source, length, offset = jnp.int32(0), jnp.int32(0), jnp.int32(0)
            for c in range(ranks.shape[0]):
                hit = ranks[c] == rank
                source = jnp.where(hit, c, source)
                length = jnp.where(hit, lengths[c], length)
                offset = jnp.where(hit, offsets[c], offset)
            home = source // cands
            at = 4 + (w * 2 + dx) * FIELDS
            info[at] = (home % 2) ^ core
            info[at + 1] = (home // 2) ^ x
            info[at + 2] = source % cands
            info[at + 3] = length
            info[at + 4] = offset


def own_head():
    return lax.axis_index("cand") // 2 * 2 + lax.axis_index("seq") % 2


def pack_keys_kernel(rk, rv, *outs):
    own = own_head()
    for d, out in enumerate(outs):
        lane = pl.ds(pl.multiple_of((own ^ d) * HEAD, HEAD), HEAD)
        out[:, :, :HEAD] = rk[:, :, lane]
        out[:, :, HEAD:] = rv[:, :, lane]


def pack_prompt_kernel(rings, *refs):
    pieces, outs = refs[:rings], refs[rings:]
    own = own_head()
    rows, width = pieces[0].shape
    for d, out in enumerate(outs):
        lane = pl.multiple_of((own ^ d) * HEAD, HEAD)
        for k, piece in enumerate(pieces):
            out[k * rows : (k + 1) * rows, :HEAD] = piece[:, pl.ds(lane, HEAD)]
            out[k * rows : (k + 1) * rows, HEAD:] = piece[:, pl.ds(lane + width // 2, HEAD)]


def pack_queries_kernel(q, *outs):
    own = own_head()
    for d, out in enumerate(outs):
        lane = pl.ds(pl.multiple_of((own ^ d) * WIDE, HEAD), WIDE)
        for w in range(q.shape[0]):
            out[w] = q[w, :, lane]


def unit_info(info, unit, field):
    return info[4 + unit * FIELDS + field]


def fetch(info, unit, dy, pieces):
    away, home, slot = (unit_info(info, unit, n) for n in range(3))
    near = jnp.where(home == 1, pieces[2 + dy][slot], pieces[dy][slot])
    far = jnp.where(home == 1, pieces[6 + dy][slot], pieces[4 + dy][slot])
    return jnp.where(away == 1, far, near)


def select_keys_kernel(info, *refs):
    pieces, outs = refs[:8], refs[8:]
    for w, out in enumerate(outs):
        for dx in range(2):
            for dy in range(2):
                out[dx, dy] = fetch(info, w * 2 + dx, dy, pieces)


def load_queries(info, unit, asked, q_all):
    rows = asked[0].shape[1]
    for dy in range(2):
        block = fetch(info, unit, dy, asked)
        for g in range(GROUP):
            at = (g * 2 + dy) * rows
            q_all[at : at + rows, :] = block[:, g * HEAD : (g + 1) * HEAD]


def online_step(q, k, v, mask, state):
    top, total, mixed = state
    scores = lax.dot_general(k, q, (((1,), (1,)), ((), ())), preferred_element_type=jnp.float32)
    scores = scores * SCORE_FACTOR
    if mask is not None:
        scores = jnp.where(mask, scores, LOWEST)
    new_top = jnp.maximum(top, jnp.max(scores, axis=0, keepdims=True))
    scale = jnp.exp2(top - new_top)
    weights = jnp.exp2(scores - new_top)
    total = total * scale + jnp.sum(weights, axis=0, keepdims=True)
    mixed = mixed * scale + lax.dot_general(
        v, weights.astype(jnp.bfloat16), (((0,), (0,)), ((), ())),
        preferred_element_type=jnp.float32,
    )
    return new_top, total, mixed


def prompt_kernel(layout, slots, chunk, info, *refs):
    asked, prompt = refs[:8], refs[8:16]
    mixed_ref, top_ref, total_ref, k_all, v_all, q_all = refs[16:]
    x, core, r, y = info[0], info[1], info[2], info[3]
    rows = prompt[0].shape[0] // layout.rings
    queries = q_all.shape[0]
    for o in range(2):
        for k in range(layout.rings):
            for d in range(4):
                piece = prompt[o * 4 + d]
                group = (x ^ (d >> 1)) * 2 + (core ^ o)
                seq = lax.rem(r + layout.rings - k, layout.rings) * 2 + (y ^ (d & 1))
                at = pl.multiple_of((group * layout.rings * 2 + seq) * rows, rows)
                here = k * rows
                k_all[pl.ds(at, rows), :] = piece[here : here + rows, :HEAD]
                v_all[pl.ds(at, rows), :] = piece[here : here + rows, HEAD:]
    for n, unit in enumerate(slots):
        length, offset = unit_info(info, unit, 3), unit_info(info, unit, 4)

        @pl.when(r * (queries // GROUP) < length)
        def _():
            load_queries(info, unit, asked, q_all)

            def run(step, state, masked):
                at = pl.multiple_of(step * chunk, chunk)
                mask = None
                if masked:
                    place = lax.broadcasted_iota(jnp.int32, (chunk, queries), 0) + at
                    mask = place < offset
                return online_step(
                    q_all[...], k_all[pl.ds(at, chunk), :], v_all[pl.ds(at, chunk), :], mask, state
                )

            state = (
                jnp.full((1, queries), LOWEST, jnp.float32),
                jnp.zeros((1, queries), jnp.float32),
                jnp.zeros((HEAD, queries), jnp.float32),
            )
            whole = offset // chunk
            state = lax.fori_loop(0, whole, lambda i, s: run(i, s, False), state)
            top_ref[n], total_ref[n], mixed_ref[n] = state

            @pl.when(whole * chunk < offset)
            def _():
                state = run(whole, (top_ref[n], total_ref[n], mixed_ref[n]), True)
                top_ref[n], total_ref[n], mixed_ref[n] = state


def query_places(first, swap, rows, queries):
    column = lax.broadcasted_iota(jnp.int32, (1, queries), 1)
    for g in range(GROUP - 1, 0, -1):
        column = jnp.where(column >= g * 2 * rows, column - g * 2 * rows, column)
    second = column >= rows
    row = jnp.where(second, column - rows, column)
    upper = jnp.where(second, 1 - swap, swap)
    return first + upper * rows + row


def response_kernel(layout, w, chunk, info, *refs):
    asked, (mixed, top, total) = refs[:8], refs[8:11]
    pieces = refs[11 : 11 + layout.rings]
    outs = refs[11 + layout.rings : 15 + layout.rings]
    k_all, v_all, q_all = refs[15 + layout.rings :]
    r, y = info[2], info[3]
    rows = outs[0].shape[0]
    queries = q_all.shape[0]
    for dx in range(2):
        unit = w * 2 + dx
        length = unit_info(info, unit, 3)

        @pl.when(r * (2 * rows) >= length)
        def _():
            for dy in range(2):
                outs[dx * 2 + dy][...] = jnp.zeros((rows, WIDE), jnp.bfloat16)

        @pl.when(r * (2 * rows) < length)
        def _():
            load_queries(info, unit, asked, q_all)
            for k, piece in enumerate(pieces):
                for dy in range(2):
                    seq = lax.rem(r + layout.rings - k, layout.rings) * 2 + (y ^ dy)
                    at = pl.multiple_of(seq * rows, rows)
                    k_all[pl.ds(at, rows), :] = piece[dx, dy, :, :HEAD]
                    v_all[pl.ds(at, rows), :] = piece[dx, dy, :, HEAD:]
            place = query_places(r * (2 * rows), y, rows, queries)

            def run(step, state):
                at = pl.multiple_of(step * chunk, chunk)
                key = lax.broadcasted_iota(jnp.int32, (chunk, queries), 0) + at
                mask = key <= jnp.minimum(place, length - 1)
                return online_step(
                    q_all[...], k_all[pl.ds(at, chunk), :], v_all[pl.ds(at, chunk), :], mask, state
                )

            last = jnp.minimum((r + 1) * 2 * rows, length)
            state = (top[dx], total[dx], mixed[dx])
            _, sums, out = lax.fori_loop(0, (last + chunk - 1) // chunk, run, state)
            out = jnp.where(place < length, out / sums, 0.0).T
            for dy in range(2):
                for g in range(GROUP):
                    at = (g * 2 + dy) * rows
                    part = out[at : at + rows].astype(jnp.bfloat16)
                    outs[dx * 2 + dy][:, g * HEAD : (g + 1) * HEAD] = part


def join_kernel(*refs):
    pieces, out = refs[:-1], refs[-1]
    own = own_head()
    for w in range(out.shape[0]):
        for d in range(4):
            lane = pl.ds(pl.multiple_of((own ^ d) * WIDE, HEAD), WIDE)
            out[w, :, lane] = pieces[w * 4 + d][...]


def divisor(total, *choices):
    for choice in choices:
        if total % choice == 0:
            return choice
    return total


def struct(*shape, dtype=jnp.bfloat16):
    return jax.ShapeDtypeStruct(shape, dtype)


def after(value, *others):
    return lax.optimization_barrier((value, *others))[0]


def body(layout, q, rk, rv, pk, pv, lengths, offsets, ranks):
    cands, rows = q.shape[0], q.shape[1]
    queries = 2 * rows * GROUP
    bf16 = functools.partial(pltpu.VMEM, dtype=jnp.bfloat16)

    def both_cores(pieces):
        return pieces + [layout.permute(piece, core=1) for piece in pieces]

    info = pl.pallas_call(
        functools.partial(plan_kernel, cands),
        out_shape=struct(4 + 2 * cands * FIELDS, dtype=jnp.int32),
        in_specs=[SMEM] * 3,
        out_specs=SMEM,
        name="plan",
    )(lengths, offsets, ranks)
    prompt = layout.ring_gather(jnp.concatenate([pk, pv], axis=1))
    keys = kernel_call(
        pack_keys_kernel, [struct(cands, rows, 2 * HEAD)] * 4, (rk, rv), name="pack_keys", scalars=0
    )
    keys = layout.exchange(keys)
    asked = kernel_call(
        pack_queries_kernel,
        [struct(cands, rows, WIDE)] * 4,
        (after(q, *keys),),
        name="pack_queries",
        scalars=0,
    )
    keys = both_cores(keys)
    slots = kernel_call(
        select_keys_kernel,
        [struct(2, 2, rows, 2 * HEAD)] * cands,
        (info, *keys),
        name="select_keys",
    )
    pieces = [layout.ring_gather(slots[0])]
    prompt = kernel_call(
        functools.partial(pack_prompt_kernel, layout.rings),
        [struct(layout.rings * pk.shape[0], 2 * HEAD)] * 4,
        prompt,
        name="pack_prompt",
        scalars=0,
    )
    prompt = both_cores(layout.exchange(prompt))
    asked = both_cores(layout.exchange(asked))
    for w in range(1, cands):
        pieces.append(layout.ring_gather(after(slots[w], *prompt)))

    prompt_keys = 8 * prompt[0].shape[0]
    chunk = divisor(prompt_keys, 512, 256, 128)
    finished = []
    for w in range(cands):
        units = (w * 2, w * 2 + 1)
        state = kernel_call(
            functools.partial(prompt_kernel, layout, units, chunk),
            [
                struct(2, HEAD, queries, dtype=jnp.float32),
                struct(2, 1, queries, dtype=jnp.float32),
                struct(2, 1, queries, dtype=jnp.float32),
            ],
            (info, *asked, *prompt),
            scratch=[bf16((prompt_keys, HEAD))] * 2 + [bf16((queries, HEAD))],
            cost=(8 * queries * prompt_keys * HEAD, 4 * prompt_keys * HEAD),
            name="prompt_part",
            spare=12 << 20,
        )
        response_keys = layout.rings * 2 * rows
        outs = kernel_call(
            functools.partial(response_kernel, layout, w, divisor(response_keys, 384, 256, 128)),
            [struct(rows, WIDE)] * 4,
            (info, *asked, *state, *pieces[w]),
            scratch=[bf16((response_keys, HEAD))] * 2 + [bf16((queries, HEAD))],
            cost=(8 * queries * response_keys * HEAD, 4 * response_keys * HEAD),
            name="response_part",
            spare=12 << 20,
        )
        finished += layout.exchange(outs)
    return kernel_call(
        join_kernel, struct(*q.shape), finished, name="join_heads", scalars=0
    )


def solution(mesh):
    in_specs = (
        P("cand", "seq", None),
        P("cand", "seq", None),
        P("cand", "seq", None),
        P(("cand", "seq"), None),
        P(("cand", "seq"), None),
        P(),
        P(),
        P(),
    )
    return jax.shard_map(
        functools.partial(body, Layout(mesh)),
        mesh=mesh,
        in_specs=in_specs,
        out_specs=P("cand", "seq", None),
        check_vma=False,
    )
```

```python
import functools
import math

import jax
import jax.numpy as jnp
from jax import lax
from jax.experimental import pallas as pl
from jax.experimental.pallas import tpu as pltpu
from jax.sharding import PartitionSpec as P

QUERY_HEADS = 20
KEY_VALUE_HEADS = 4
HEAD = 128
GROUP = QUERY_HEADS // KEY_VALUE_HEADS
WIDE = GROUP * HEAD
SCORE_FACTOR = math.log2(math.e) / math.sqrt(HEAD)
LOWEST = -1e30
AXES = ("cand", "seq")
VMEM = pl.BlockSpec(memory_space=pltpu.VMEM)
SMEM = pl.BlockSpec(memory_space=pltpu.SMEM)

FIELDS = 5


class Layout:
    def __init__(self, mesh):
        assert mesh.shape["cand"] == 4 and mesh.shape["seq"] % 2 == 0
        self.rings = mesh.shape["seq"] // 2

    def permute(self, array, d=0, core=0, ring=0):
        pairs = []
        for x in range(2):
            for c in range(2):
                for r in range(self.rings):
                    for y in range(2):
                        source = ((x * 2 + c) * self.rings + r) * 2 + y
                        target = ((x ^ (d >> 1)) * 2 + (c ^ core)) * self.rings
                        target = (target + (r + ring) % self.rings) * 2 + (y ^ (d & 1))
                        pairs.append((source, target))
        return lax.ppermute(array, AXES, pairs)

    def exchange(self, pieces):
        return [pieces[0]] + [self.permute(pieces[d], d=d) for d in range(1, 4)]

    def spread(self, block):
        return [block] + [self.permute(block, ring=k) for k in range(1, self.rings)]

    def ring_gather(self, block):
        pieces = [block]
        for _ in range(self.rings - 1):
            pieces.append(self.permute(pieces[-1], ring=1))
        return pieces


def kernel_call(kernel, out_shape, operands, scratch=(), cost=(0, 0), name=None, scalars=1, spare=2 << 20):
    many = isinstance(out_shape, list)
    arrays = list(operands) + (list(out_shape) if many else [out_shape]) + list(scratch)
    held = sum(math.prod(a.shape) * jnp.dtype(a.dtype).itemsize for a in arrays)
    return pl.pallas_call(
        kernel,
        out_shape=out_shape,
        in_specs=[SMEM] * scalars + [VMEM] * (len(operands) - scalars),
        out_specs=[VMEM] * len(out_shape) if many else VMEM,
        scratch_shapes=list(scratch),
        compiler_params=pltpu.CompilerParams(vmem_limit_bytes=held + held // 4 + spare),
        cost_estimate=pl.CostEstimate(
            flops=cost[0], transcendentals=cost[0] // 512, bytes_accessed=cost[1]
        ),
        name=name,
    )(*operands)


def plan_kernel(cands, lengths, offsets, ranks, info):
    group, seq = lax.axis_index("cand"), lax.axis_index("seq")
    x, core = group // 2, group % 2
    info[0], info[1], info[2], info[3] = x, core, seq // 2, seq % 2
    for w in range(cands):
        for dx in range(2):
            rank = ((x ^ dx) * 2 + core) * cands + w
            source, length, offset = jnp.int32(0), jnp.int32(0), jnp.int32(0)
            for c in range(ranks.shape[0]):
                hit = ranks[c] == rank
                source = jnp.where(hit, c, source)
                length = jnp.where(hit, lengths[c], length)
                offset = jnp.where(hit, offsets[c], offset)
            home = source // cands
            at = 4 + (w * 2 + dx) * FIELDS
            info[at] = (home % 2) ^ core
            info[at + 1] = (home // 2) ^ x
            info[at + 2] = source % cands
            info[at + 3] = length
            info[at + 4] = offset


def own_head():
    return lax.axis_index("cand") // 2 * 2 + lax.axis_index("seq") % 2


def pack_keys_kernel(rk, rv, *outs):
    own = own_head()
    cands, rows = rk.shape[0], rk.shape[1]
    for d, out in enumerate(outs):
        lane = pl.ds(pl.multiple_of((own ^ d) * HEAD, HEAD), HEAD)
        for w in range(cands):
            out[w * rows : (w + 1) * rows, :HEAD] = rk[w, :, lane]
            out[w * rows : (w + 1) * rows, HEAD:] = rv[w, :, lane]


def pack_kernel(rings, q, *refs):
    pieces, outs = refs[:rings], refs[rings:]
    own = own_head()
    cands, rows = q.shape[0], q.shape[1]
    prompt_rows, width = pieces[0].shape
    for d, out in enumerate(outs):
        for w in range(cands):
            for g in range(GROUP):
                lane = pl.multiple_of((own ^ d) * WIDE + g * HEAD, HEAD)
                at = (w * GROUP + g) * rows
                out[at : at + rows, :] = q[w, :, pl.ds(lane, HEAD)]
        for half in range(2):
            lane = pl.multiple_of((own ^ d) * HEAD + half * (width // 2), HEAD)
            for k, piece in enumerate(pieces):
                at = cands * GROUP * rows + (half * rings + k) * prompt_rows
                out[at : at + prompt_rows, :] = piece[:, pl.ds(lane, HEAD)]


def unit_info(info, unit, field):
    return info[4 + unit * FIELDS + field]


def fetch(info, unit, dy, pieces, row, rows):
    away, home = unit_info(info, unit, 0), unit_info(info, unit, 1)
    at = pl.ds(pl.multiple_of(row, rows), rows)
    near = jnp.where(home == 1, pieces[2 + dy][at, :], pieces[dy][at, :])
    far = jnp.where(home == 1, pieces[6 + dy][at, :], pieces[4 + dy][at, :])
    return jnp.where(away == 1, far, near)


def select_keys_kernel(info, *refs):
    pieces, outs = refs[:8], refs[8:]
    rows = outs[0].shape[2]
    for w, out in enumerate(outs):
        for dx in range(2):
            unit = w * 2 + dx
            for dy in range(2):
                out[dx, dy] = fetch(info, unit, dy, pieces, unit_info(info, unit, 2) * rows, rows)


def load_queries(info, unit, packed, q_all):
    rows = q_all.shape[0] // (2 * GROUP)
    for dy in range(2):
        for g in range(GROUP):
            row = (unit_info(info, unit, 2) * GROUP + g) * rows
            at = (g * 2 + dy) * rows
            q_all[at : at + rows, :] = fetch(info, unit, dy, packed, row, rows)


def online_step(q, k, v, mask, state):
    top, total, mixed = state
    scores = lax.dot_general(k, q, (((1,), (1,)), ((), ())), preferred_element_type=jnp.float32)
    scores = scores * SCORE_FACTOR
    if mask is not None:
        scores = jnp.where(mask, scores, LOWEST)
    new_top = jnp.maximum(top, jnp.max(scores, axis=0, keepdims=True))
    scale = jnp.exp2(top - new_top)
    weights = jnp.exp2(scores - new_top)
    total = total * scale + jnp.sum(weights, axis=0, keepdims=True)
    mixed = mixed * scale + lax.dot_general(
        v, weights.astype(jnp.bfloat16), (((0,), (0,)), ((), ())),
        preferred_element_type=jnp.float32,
    )
    return new_top, total, mixed


def prompt_kernel(layout, slots, chunk, info, *refs):
    packed = refs[:8]
    mixed_ref, top_ref, total_ref, k_all, v_all, q_all = refs[8:]
    x, core, r, y = info[0], info[1], info[2], info[3]
    rows = k_all.shape[0] // (layout.rings * 8)
    queries = q_all.shape[0]
    first = packed[0].shape[0] - 2 * layout.rings * rows
    for o in range(2):
        for k in range(layout.rings):
            for d in range(4):
                piece = packed[o * 4 + d]
                group = (x ^ (d >> 1)) * 2 + (core ^ o)
                seq = lax.rem(r + layout.rings - k, layout.rings) * 2 + (y ^ (d & 1))
                at = pl.multiple_of((group * layout.rings * 2 + seq) * rows, rows)
                here = first + k * rows
                k_all[pl.ds(at, rows), :] = piece[here : here + rows, :]
                here += layout.rings * rows
                v_all[pl.ds(at, rows), :] = piece[here : here + rows, :]
    for n, unit in enumerate(slots):
        length, offset = unit_info(info, unit, 3), unit_info(info, unit, 4)

        @pl.when(r * (queries // GROUP) < length)
        def _():
            load_queries(info, unit, packed, q_all)

            def run(step, state, masked):
                at = pl.multiple_of(step * chunk, chunk)
                mask = None
                if masked:
                    place = lax.broadcasted_iota(jnp.int32, (chunk, queries), 0) + at
                    mask = place < offset
                return online_step(
                    q_all[...], k_all[pl.ds(at, chunk), :], v_all[pl.ds(at, chunk), :], mask, state
                )

            state = (
                jnp.full((1, queries), LOWEST, jnp.float32),
                jnp.zeros((1, queries), jnp.float32),
                jnp.zeros((HEAD, queries), jnp.float32),
            )
            whole = offset // chunk
            state = lax.fori_loop(0, whole, lambda i, s: run(i, s, False), state)
            top_ref[n], total_ref[n], mixed_ref[n] = state

            @pl.when(whole * chunk < offset)
            def _():
                state = run(whole, (top_ref[n], total_ref[n], mixed_ref[n]), True)
                top_ref[n], total_ref[n], mixed_ref[n] = state


def query_places(first, swap, rows, queries):
    column = lax.broadcasted_iota(jnp.int32, (1, queries), 1)
    for g in range(GROUP - 1, 0, -1):
        column = jnp.where(column >= g * 2 * rows, column - g * 2 * rows, column)
    second = column >= rows
    row = jnp.where(second, column - rows, column)
    upper = jnp.where(second, 1 - swap, swap)
    return first + upper * rows + row


def response_kernel(layout, w, dx, chunk, info, *refs):
    packed, (mixed, top, total) = refs[:8], refs[8:11]
    pieces = refs[11 : 11 + layout.rings]
    outs = refs[11 + layout.rings : 13 + layout.rings]
    k_all, v_all, q_all = refs[13 + layout.rings :]
    r, y = info[2], info[3]
    rows = outs[0].shape[0]
    queries = q_all.shape[0]
    unit = w * 2 + dx
    length = unit_info(info, unit, 3)

    @pl.when(r * (2 * rows) >= length)
    def _():
        for out in outs:
            out[...] = jnp.zeros(out.shape, out.dtype)

    @pl.when(r * (2 * rows) < length)
    def _():
        load_queries(info, unit, packed, q_all)
        for k, piece in enumerate(pieces):
            for dy in range(2):
                seq = lax.rem(r + layout.rings - k, layout.rings) * 2 + (y ^ dy)
                at = pl.multiple_of(seq * rows, rows)
                k_all[pl.ds(at, rows), :] = piece[dx, dy, :, :HEAD]
                v_all[pl.ds(at, rows), :] = piece[dx, dy, :, HEAD:]
        place = query_places(r * (2 * rows), y, rows, queries)

        def run(step, state):
            at = pl.multiple_of(step * chunk, chunk)
            key = lax.broadcasted_iota(jnp.int32, (chunk, queries), 0) + at
            mask = key <= jnp.minimum(place, length - 1)
            return online_step(
                q_all[...], k_all[pl.ds(at, chunk), :], v_all[pl.ds(at, chunk), :], mask, state
            )

        last = jnp.minimum((r + 1) * 2 * rows, length)
        state = (top[dx], total[dx], mixed[dx])
        _, sums, result = lax.fori_loop(0, (last + chunk - 1) // chunk, run, state)
        result = jnp.where(place < length, result / sums, 0.0).T
        for dy, out in enumerate(outs):
            for g in range(GROUP):
                at = (g * 2 + dy) * rows
                part = result[at : at + rows].astype(jnp.bfloat16)
                out[:, g * HEAD : (g + 1) * HEAD] = part


def join_kernel(*refs):
    pieces, out = refs[:-1], refs[-1]
    own = own_head()
    for w in range(out.shape[0]):
        for d in range(4):
            lane = pl.ds(pl.multiple_of((own ^ d) * WIDE, HEAD), WIDE)
            out[w, :, lane] = pieces[w * 4 + d][...]


def divisor(total, *choices):
    for choice in choices:
        if total % choice == 0:
            return choice
    return total


def struct(*shape, dtype=jnp.bfloat16):
    return jax.ShapeDtypeStruct(shape, dtype)


def after(value, *others):
    return lax.optimization_barrier((value, *others))[0]


def body(layout, q, rk, rv, pk, pv, lengths, offsets, ranks):
    cands, rows = q.shape[0], q.shape[1]
    queries = 2 * rows * GROUP
    bf16 = functools.partial(pltpu.VMEM, dtype=jnp.bfloat16)

    def both_cores(pieces):
        return pieces + [layout.permute(piece, core=1) for piece in pieces]

    info = pl.pallas_call(
        functools.partial(plan_kernel, cands),
        out_shape=struct(4 + 2 * cands * FIELDS, dtype=jnp.int32),
        in_specs=[SMEM] * 3,
        out_specs=SMEM,
        name="plan",
    )(lengths, offsets, ranks)
    prompt = layout.spread(jnp.concatenate([pk, pv], axis=1))
    keys = kernel_call(
        pack_keys_kernel, [struct(cands * rows, 2 * HEAD)] * 4, (rk, rv), name="pack_keys", scalars=0
    )
    keys = both_cores(layout.exchange(keys))
    slots = kernel_call(
        select_keys_kernel,
        [struct(2, 2, rows, 2 * HEAD)] * cands,
        (info, *keys),
        name="select_keys",
    )
    pieces = [layout.ring_gather(slots[0])]
    prompt_rows = layout.rings * pk.shape[0]
    packed = kernel_call(
        functools.partial(pack_kernel, layout.rings),
        [struct(cands * GROUP * rows + 2 * prompt_rows, HEAD)] * 4,
        (after(q, slots[0]), *prompt),
        name="pack_queries_prompt",
        scalars=0,
    )
    packed = both_cores(layout.exchange(packed))
    for w in range(1, cands):
        pieces.append(layout.spread(after(slots[w], *packed)))

    prompt_keys = 8 * prompt_rows
    response_keys = layout.rings * 2 * rows
    chunk = divisor(prompt_keys, 512, 256, 128)
    finished = []
    for w in range(cands):
        state = kernel_call(
            functools.partial(prompt_kernel, layout, (w * 2, w * 2 + 1), chunk),
            [
                struct(2, HEAD, queries, dtype=jnp.float32),
                struct(2, 1, queries, dtype=jnp.float32),
                struct(2, 1, queries, dtype=jnp.float32),
            ],
            (info, *packed),
            scratch=[bf16((prompt_keys, HEAD))] * 2 + [bf16((queries, HEAD))],
            cost=(8 * queries * prompt_keys * HEAD, 4 * prompt_keys * HEAD),
            name="prompt_part",
            spare=12 << 20,
        )
        outs = [None] * 4
        for dx in (1, 0):
            outs[dx * 2], outs[dx * 2 + 1] = kernel_call(
                functools.partial(
                    response_kernel, layout, w, dx, divisor(response_keys, 384, 256, 128)
                ),
                [struct(rows, WIDE)] * 2,
                (info, *packed, *state, *pieces[w]),
                scratch=[bf16((response_keys, HEAD))] * 2 + [bf16((queries, HEAD))],
                cost=(4 * queries * response_keys * HEAD, 2 * response_keys * HEAD),
                name="response_part",
                spare=12 << 20,
            )
        finished += layout.exchange(outs)
    return kernel_call(join_kernel, struct(*q.shape), finished, name="join_heads", scalars=0)


def solution(mesh):
    in_specs = (
        P("cand", "seq", None),
        P("cand", "seq", None),
        P("cand", "seq", None),
        P(("cand", "seq"), None),
        P(("cand", "seq"), None),
        P(),
        P(),
        P(),
    )
    return jax.shard_map(
        functools.partial(body, Layout(mesh)),
        mesh=mesh,
        in_specs=in_specs,
        out_specs=P("cand", "seq", None),
        check_vma=False,
    )
```

```python
import functools
import math

import jax
import jax.numpy as jnp
from jax import lax
from jax.experimental import pallas as pl
from jax.experimental.pallas import tpu as pltpu
from jax.sharding import PartitionSpec as P

QUERY_HEADS = 20
KEY_VALUE_HEADS = 4
HEAD = 128
GROUP = QUERY_HEADS // KEY_VALUE_HEADS
WIDE = GROUP * HEAD
SCORE_FACTOR = math.log2(math.e) / math.sqrt(HEAD)
LOWEST = -1e30
AXES = ("cand", "seq")
PACK_VMEM = 60 << 20
VMEM = pl.BlockSpec(memory_space=pltpu.VMEM)
SMEM = pl.BlockSpec(memory_space=pltpu.SMEM)


class Layout:
    def __init__(self, mesh):
        assert mesh.shape["cand"] == 4 and mesh.shape["seq"] % 2 == 0
        self.rings = mesh.shape["seq"] // 2

    def permute(self, array, d=0, core=0, ring=0):
        pairs = []
        for x in range(2):
            for c in range(2):
                for r in range(self.rings):
                    for y in range(2):
                        source = ((x * 2 + c) * self.rings + r) * 2 + y
                        target = ((x ^ (d >> 1)) * 2 + (c ^ core)) * self.rings
                        target = (target + (r + ring) % self.rings) * 2 + (y ^ (d & 1))
                        pairs.append((source, target))
        return lax.ppermute(array, AXES, pairs)

    def exchange(self, pieces):
        return [pieces[0]] + [self.permute(pieces[d], d=d) for d in range(1, 4)]

    def spread(self, block):
        return [block] + [self.permute(block, ring=k) for k in range(1, self.rings)]

    def ring_gather(self, block):
        pieces = [block]
        for _ in range(self.rings - 1):
            pieces.append(self.permute(pieces[-1], ring=1))
        return pieces


def kernel_call(kernel, out_shape, operands, scratch=(), cost=(0, 0), name=None, scalars=1, spare=2 << 20):
    many = isinstance(out_shape, list)
    arrays = list(operands) + (list(out_shape) if many else [out_shape]) + list(scratch)
    held = sum(math.prod(a.shape) * jnp.dtype(a.dtype).itemsize for a in arrays)
    return pl.pallas_call(
        kernel,
        out_shape=out_shape,
        in_specs=[SMEM] * scalars + [VMEM] * (len(operands) - scalars),
        out_specs=[VMEM] * len(out_shape) if many else VMEM,
        scratch_shapes=list(scratch),
        compiler_params=pltpu.CompilerParams(vmem_limit_bytes=held + held // 4 + spare),
        cost_estimate=pl.CostEstimate(
            flops=cost[0], transcendentals=cost[0] // 512, bytes_accessed=cost[1]
        ),
        name=name,
    )(*operands)


def own_head():
    return lax.axis_index("cand") // 2 * 2 + lax.axis_index("seq") % 2


def pack_first_kernel(rk, rv, pk, pv, *refs):
    outs, joined, sems = refs[:4], refs[4], refs[5]
    own = own_head()
    cands, rows = rk.shape[0], rk.shape[1]
    moves = []
    width = pk.shape[1]
    for half, source in enumerate((pk, pv)):
        moves.append((source, joined.at[:, pl.ds(half * width, width)]))
    for d, out in enumerate(outs):
        lane = pl.ds(pl.multiple_of((own ^ d) * HEAD, HEAD), HEAD)
        for half, source in enumerate((rk, rv)):
            for w in range(cands):
                target = out.at[pl.ds(w * rows, rows), pl.ds(half * HEAD, HEAD)]
                moves.append((source.at[w, :, lane], target))
    copies = [pltpu.make_async_copy(a, b, sems.at[n]) for n, (a, b) in enumerate(moves)]
    for copy in copies:
        copy.start()
    for copy in copies:
        copy.wait()


def pack_kernel(rings, q, *refs):
    pieces, outs = refs[:rings], refs[rings:]
    own = own_head()
    cands, rows = q.shape[0], q.shape[1]
    prompt_rows, width = pieces[0].shape
    for d, out in enumerate(outs):
        for w in range(cands):
            for g in range(GROUP):
                lane = pl.multiple_of((own ^ d) * WIDE + g * HEAD, HEAD)
                at = (w * GROUP + g) * rows
                out[at : at + rows, :] = q[w, :, pl.ds(lane, HEAD)]
        for half in range(2):
            lane = pl.multiple_of((own ^ d) * HEAD + half * (width // 2), HEAD)
            for k, piece in enumerate(pieces):
                at = cands * GROUP * rows + (half * rings + k) * prompt_rows
                out[at : at + prompt_rows, :] = piece[:, pl.ds(lane, HEAD)]


def stack_kernel(*refs):
    for n, piece in enumerate(refs[:-1]):
        refs[-1][n] = piece[...]


def unit_facts(facts, w, dx):
    group, count = lax.axis_index("cand"), facts.shape[0] // 3
    x, core = group // 2, group % 2
    cands = count // 4
    rank = ((x ^ dx) * 2 + core) * cands + w
    source = jnp.int32(0)
    for c in range(count):
        source = jnp.where(facts[2 * count + c] == rank, c, source)
    home = source // cands
    away = (home % 2) ^ core
    return away, (home // 2) ^ x, source % cands, facts[source], facts[count + source]


def fetch(unit, dy, own, other, row, rows):
    d = unit[1] * 2 + dy
    at = pl.ds(pl.multiple_of(row, rows), rows)
    return jnp.where(unit[0] == 1, other[d, at, :], own[d, at, :])


def select_keys_kernel(facts, own, other, *outs):
    rows = outs[0].shape[2]
    for w, out in enumerate(outs):
        for dx in range(2):
            unit = unit_facts(facts, w, dx)
            for dy in range(2):
                out[dx, dy] = fetch(unit, dy, own, other, unit[2] * rows, rows)


def load_queries(unit, own, other, q_all):
    rows = q_all.shape[0] // (2 * GROUP)
    for dy in range(2):
        for g in range(GROUP):
            row = (unit[2] * GROUP + g) * rows
            at = (g * 2 + dy) * rows
            q_all[at : at + rows, :] = fetch(unit, dy, own, other, row, rows)


def online_step(q, k, v, mask, state):
    top, total, mixed = state
    scores = lax.dot_general(k, q, (((1,), (1,)), ((), ())), preferred_element_type=jnp.float32)
    scores = scores * SCORE_FACTOR
    if mask is not None:
        scores = jnp.where(mask, scores, LOWEST)
    new_top = jnp.maximum(top, jnp.max(scores, axis=0, keepdims=True))
    scale = jnp.exp2(top - new_top)
    weights = jnp.exp2(scores - new_top)
    total = total * scale + jnp.sum(weights, axis=0, keepdims=True)
    mixed = mixed * scale + lax.dot_general(
        v, weights.astype(jnp.bfloat16), (((0,), (0,)), ((), ())),
        preferred_element_type=jnp.float32,
    )
    return new_top, total, mixed


def device_place():
    group, seq = lax.axis_index("cand"), lax.axis_index("seq")
    return group // 2, group % 2, seq // 2, seq % 2


def prompt_kernel(layout, w, chunk, facts, own, other, *refs):
    mixed_ref, top_ref, total_ref, k_all, v_all, q_all = refs
    x, core, r, y = device_place()
    rows = k_all.shape[0] // (8 * layout.rings)
    queries = q_all.shape[0]
    first = own.shape[1] - 2 * layout.rings * rows
    for o, piece in enumerate((own, other)):
        for k in range(layout.rings):
            for d in range(4):
                group = (x ^ (d >> 1)) * 2 + (core ^ o)
                seq = lax.rem(r + layout.rings - k, layout.rings) * 2 + (y ^ (d & 1))
                at = pl.multiple_of((group * layout.rings * 2 + seq) * rows, rows)
                for half, target in enumerate((k_all, v_all)):
                    here = first + (half * layout.rings + k) * rows
                    target[pl.ds(at, rows), :] = piece[d, here : here + rows, :]
    for n in range(2):
        unit = unit_facts(facts, w, n)
        length, offset = unit[3], unit[4]

        @pl.when(r * (queries // GROUP) < length)
        def _():
            load_queries(unit, own, other, q_all)

            def run(at, size, state, masked):
                mask = None
                if masked:
                    place = lax.broadcasted_iota(jnp.int32, (size, queries), 0) + at
                    mask = place < offset
                return online_step(
                    q_all[...], k_all[pl.ds(at, size), :], v_all[pl.ds(at, size), :], mask, state
                )

            def whole(i, state):
                return run(pl.multiple_of(i * chunk, chunk), chunk, state, False)

            def part(i, state):
                return run(pl.multiple_of(i * (chunk // 2), chunk // 2), chunk // 2, state, True)

            state = (
                jnp.full((1, queries), LOWEST, jnp.float32),
                jnp.zeros((1, queries), jnp.float32),
                jnp.zeros((HEAD, queries), jnp.float32),
            )
            count = offset // chunk
            state = lax.fori_loop(0, count, whole, state)
            end = (offset + chunk // 2 - 1) // (chunk // 2)
            state = lax.fori_loop(count * 2, end, part, state)
            top_ref[n], total_ref[n], mixed_ref[n] = state


def query_places(first, swap, rows, queries):
    column = lax.broadcasted_iota(jnp.int32, (1, queries), 1)
    for g in range(GROUP - 1, 0, -1):
        column = jnp.where(column >= g * 2 * rows, column - g * 2 * rows, column)
    second = column >= rows
    row = jnp.where(second, column - rows, column)
    upper = jnp.where(second, 1 - swap, swap)
    return first + upper * rows + row


def response_kernel(layout, w, dx, facts, own, other, mixed, top, total, *refs):
    pieces = refs[: layout.rings]
    outs = refs[layout.rings : 2 + layout.rings]
    k_all, v_all, q_all = refs[2 + layout.rings :]
    _, _, r, y = device_place()
    rows = outs[0].shape[0]
    queries = q_all.shape[0]
    unit = unit_facts(facts, w, dx)
    length = unit[3]

    @pl.when(r * (2 * rows) >= length)
    def _():
        for out in outs:
            out[...] = jnp.zeros(out.shape, out.dtype)

    @pl.when(r * (2 * rows) < length)
    def _():
        load_queries(unit, own, other, q_all)
        for k, piece in enumerate(pieces):
            for dy in range(2):
                seq = lax.rem(r + layout.rings - k, layout.rings) * 2 + (y ^ dy)
                at = pl.multiple_of(seq * rows, rows)
                k_all[pl.ds(at, rows), :] = piece[dx, dy, :, :HEAD]
                v_all[pl.ds(at, rows), :] = piece[dx, dy, :, HEAD:]
        place = query_places(r * (2 * rows), y, rows, queries)
        top_ref, total_ref, mixed_ref = top.at[dx], total.at[dx], mixed.at[dx]
        half = 2 * rows

        def run(at, size, state):
            at = pl.multiple_of(at, half)
            key = lax.broadcasted_iota(jnp.int32, (size, queries), 0) + at
            mask = key <= jnp.minimum(place, length - 1)
            return online_step(
                q_all[...], k_all[pl.ds(at, size), :], v_all[pl.ds(at, size), :], mask, state
            )

        last = jnp.minimum((r + 1) * half, length)
        count = (last + half - 1) // (2 * half)
        state = (top_ref[...], total_ref[...], mixed_ref[...])
        state = lax.fori_loop(
            0, count, lambda i, s: run(i * (2 * half), 2 * half, s), state
        )
        rest = (last - count * (2 * half) + half - 1) // half
        _, sums, result = lax.fori_loop(
            0, rest, lambda i, s: run(count * (2 * half), half, s), state
        )
        result = jnp.where(place < length, result / sums, 0.0).T
        for dy, out in enumerate(outs):
            for g in range(GROUP):
                at = (g * 2 + dy) * rows
                part = result[at : at + rows].astype(jnp.bfloat16)
                out[:, g * HEAD : (g + 1) * HEAD] = part


def join_kernel(*refs):
    pieces, out = refs[:-1], refs[-1]
    own = own_head()
    for w in range(out.shape[0]):
        for d in range(4):
            lane = pl.ds(pl.multiple_of((own ^ d) * WIDE, HEAD), WIDE)
            out[w, :, lane] = pieces[w * 4 + d][...]


def divisor(total, *choices):
    for choice in choices:
        if total % choice == 0:
            return choice
    return total


def struct(*shape, dtype=jnp.bfloat16):
    return jax.ShapeDtypeStruct(shape, dtype)


def after(value, *others):
    return lax.optimization_barrier((value, *others))[0]


def body(layout, q, rk, rv, pk, pv, lengths, offsets, ranks):
    cands, rows = q.shape[0], q.shape[1]
    queries = 2 * rows * GROUP
    bf16 = functools.partial(pltpu.VMEM, dtype=jnp.bfloat16)

    def exchange(pieces, *held):
        got = layout.exchange(pieces)
        if held:
            got[0] = after(got[0], *held)
        own = kernel_call(
            stack_kernel, struct(4, *got[0].shape), got, name="stack", scalars=0
        )
        return own, layout.permute(own, core=1)

    facts = jnp.concatenate([lengths, offsets, ranks])
    anywhere = pl.BlockSpec(memory_space=pl.ANY)
    *keys, prompt = pl.pallas_call(
        pack_first_kernel,
        out_shape=[struct(cands * rows, 2 * HEAD)] * 4 + [struct(pk.shape[0], 2 * pk.shape[1])],
        in_specs=[anywhere] * 4,
        out_specs=[VMEM] * 5,
        scratch_shapes=[pltpu.SemaphoreType.DMA((2 + 8 * cands,))],
        compiler_params=pltpu.CompilerParams(vmem_limit_bytes=PACK_VMEM),
        name="pack_first",
    )(rk, rv, pk, pv)
    prompt = layout.spread(prompt)
    prompt_rows = layout.rings * pk.shape[0]
    packed = kernel_call(
        functools.partial(pack_kernel, layout.rings),
        [struct(cands * GROUP * rows + 2 * prompt_rows, HEAD)] * 4,
        (q, *prompt),
        name="pack_queries_prompt",
        scalars=0,
    )
    keys, keys_other = exchange(keys, packed[0])
    slots = kernel_call(
        select_keys_kernel,
        [struct(2, 2, rows, 2 * HEAD)] * cands,
        (facts, keys, keys_other),
        name="select_keys",
    )
    pieces = [layout.spread(slots[0])]
    packed = exchange(packed, *pieces[0])
    for w in range(1, cands):
        pieces.append(layout.spread(after(slots[w], packed[0])))

    prompt_keys = 8 * prompt_rows
    response_keys = layout.rings * 2 * rows
    chunk = divisor(prompt_keys, 1024, 512, 256)
    states = []
    for w in range(cands):
        states.append(
            kernel_call(
                functools.partial(prompt_kernel, layout, w, chunk),
                [
                    struct(2, HEAD, queries, dtype=jnp.float32),
                    struct(2, 1, queries, dtype=jnp.float32),
                    struct(2, 1, queries, dtype=jnp.float32),
                ],
                (facts, *packed),
                scratch=[bf16((prompt_keys, HEAD))] * 2 + [bf16((queries, HEAD))],
                cost=(8 * queries * prompt_keys * HEAD, 4 * prompt_keys * HEAD),
                name="prompt_part",
                spare=16 << 20,
            )
        )
    finished = []
    for w in range(cands):
        outs = [None] * 4
        for dx in (1, 0):
            outs[dx * 2], outs[dx * 2 + 1] = kernel_call(
                functools.partial(response_kernel, layout, w, dx),
                [struct(rows, WIDE)] * 2,
                (facts, *packed, *states[w], *pieces[w]),
                scratch=[bf16((response_keys, HEAD))] * 2 + [bf16((queries, HEAD))],
                cost=(4 * queries * response_keys * HEAD, 2 * response_keys * HEAD),
                name="response_part",
                spare=12 << 20,
            )
        finished += layout.exchange(outs)
    return kernel_call(join_kernel, struct(*q.shape), finished, name="join_heads", scalars=0)


def solution(mesh):
    in_specs = (
        P("cand", "seq", None),
        P("cand", "seq", None),
        P("cand", "seq", None),
        P(("cand", "seq"), None),
        P(("cand", "seq"), None),
        P(),
        P(),
        P(),
    )
    return jax.shard_map(
        functools.partial(body, Layout(mesh)),
        mesh=mesh,
        in_specs=in_specs,
        out_specs=P("cand", "seq", None),
        check_vma=False,
    )
```

```python
import functools
import math

import jax
import jax.numpy as jnp
from jax import lax
from jax.experimental import pallas as pl
from jax.experimental.pallas import tpu as pltpu
from jax.sharding import PartitionSpec as P

QUERY_HEADS = 20
KEY_VALUE_HEADS = 4
HEAD = 128
GROUP = QUERY_HEADS // KEY_VALUE_HEADS
WIDE = GROUP * HEAD
SCORE_FACTOR = math.log2(math.e) / math.sqrt(HEAD)
LOWEST = -1e30
AXES = ("cand", "seq")
PACK_VMEM = 60 << 20
VMEM = pl.BlockSpec(memory_space=pltpu.VMEM)
SMEM = pl.BlockSpec(memory_space=pltpu.SMEM)


class Layout:
    def __init__(self, mesh):
        assert mesh.shape["cand"] == 4 and mesh.shape["seq"] % 2 == 0
        self.rings = mesh.shape["seq"] // 2

    def permute(self, array, d=0, core=0, ring=0):
        pairs = []
        for x in range(2):
            for c in range(2):
                for r in range(self.rings):
                    for y in range(2):
                        source = ((x * 2 + c) * self.rings + r) * 2 + y
                        target = ((x ^ (d >> 1)) * 2 + (c ^ core)) * self.rings
                        target = (target + (r + ring) % self.rings) * 2 + (y ^ (d & 1))
                        pairs.append((source, target))
        return lax.ppermute(array, AXES, pairs)

    def exchange(self, pieces):
        return [pieces[0]] + [self.permute(pieces[d], d=d) for d in range(1, 4)]

    def spread(self, block):
        return [block] + [self.permute(block, ring=k) for k in range(1, self.rings)]

    def ring_gather(self, block):
        pieces = [block]
        for _ in range(self.rings - 1):
            pieces.append(self.permute(pieces[-1], ring=1))
        return pieces


def kernel_call(kernel, out_shape, operands, scratch=(), cost=(0, 0), name=None, scalars=1, spare=2 << 20):
    many = isinstance(out_shape, list)
    arrays = list(operands) + (list(out_shape) if many else [out_shape]) + list(scratch)
    held = sum(math.prod(a.shape) * jnp.dtype(a.dtype).itemsize for a in arrays)
    return pl.pallas_call(
        kernel,
        out_shape=out_shape,
        in_specs=[SMEM] * scalars + [VMEM] * (len(operands) - scalars),
        out_specs=[VMEM] * len(out_shape) if many else VMEM,
        scratch_shapes=list(scratch),
        compiler_params=pltpu.CompilerParams(vmem_limit_bytes=held + held // 4 + spare),
        cost_estimate=pl.CostEstimate(
            flops=cost[0], transcendentals=cost[0] // 512, bytes_accessed=cost[1]
        ),
        name=name,
    )(*operands)


def own_head():
    return lax.axis_index("cand") // 2 * 2 + lax.axis_index("seq") % 2


def pack_first_kernel(rk, rv, pk, pv, *refs):
    outs, joined, sems = refs[:4], refs[4], refs[5]
    own = own_head()
    cands, rows = rk.shape[0], rk.shape[1]
    moves = []
    width = pk.shape[1]
    for half, source in enumerate((pk, pv)):
        moves.append((source, joined.at[:, pl.ds(half * width, width)]))
    for d, out in enumerate(outs):
        lane = pl.ds(pl.multiple_of((own ^ d) * HEAD, HEAD), HEAD)
        for half, source in enumerate((rk, rv)):
            for w in range(cands):
                target = out.at[pl.ds(w * rows, rows), pl.ds(half * HEAD, HEAD)]
                moves.append((source.at[w, :, lane], target))
    copies = [pltpu.make_async_copy(a, b, sems.at[n]) for n, (a, b) in enumerate(moves)]
    for copy in copies:
        copy.start()
    for copy in copies:
        copy.wait()


def pack_queries_kernel(q, *outs):
    own = own_head()
    cands, rows = q.shape[0], q.shape[1]
    for d, out in enumerate(outs):
        for w in range(cands):
            for g in range(GROUP):
                lane = pl.multiple_of((own ^ d) * WIDE + g * HEAD, HEAD)
                at = (w * GROUP + g) * rows
                out[at : at + rows, :] = q[w, :, pl.ds(lane, HEAD)]


def pack_kernel(rings, *refs):
    asked, mine, pieces, outs = refs[:4], refs[4:6], refs[6 : 5 + rings], refs[5 + rings :]
    own = own_head()
    rows, width = pieces[0].shape
    for d, out in enumerate(outs):
        first = asked[d].shape[0]
        out[:first, :] = asked[d][...]
        for half in range(2):
            lane = pl.multiple_of((own ^ d) * HEAD + half * (width // 2), HEAD)
            at = first + half * rings * rows
            mine_lane = pl.ds(pl.multiple_of((own ^ d) * HEAD, HEAD), HEAD)
            out[at : at + rows, :] = mine[half][:, mine_lane]
            for k, piece in enumerate(pieces):
                at = first + (half * rings + k + 1) * rows
                out[at : at + rows, :] = piece[:, pl.ds(lane, HEAD)]


def stack_kernel(*refs):
    for n, piece in enumerate(refs[:-1]):
        refs[-1][n] = piece[...]


def unit_facts(facts, w, dx):
    group, count = lax.axis_index("cand"), facts.shape[0] // 3
    x, core = group // 2, group % 2
    cands = count // 4
    rank = ((x ^ dx) * 2 + core) * cands + w
    source = jnp.int32(0)
    for c in range(count):
        source = jnp.where(facts[2 * count + c] == rank, c, source)
    home = source // cands
    away = (home % 2) ^ core
    return away, (home // 2) ^ x, source % cands, facts[source], facts[count + source]


def fetch(unit, dy, own, other, row, rows):
    d = unit[1] * 2 + dy
    at = pl.ds(pl.multiple_of(row, rows), rows)
    return jnp.where(unit[0] == 1, other[d, at, :], own[d, at, :])


def select_keys_kernel(facts, own, other, *outs):
    rows = outs[0].shape[2]
    for w, out in enumerate(outs):
        for dx in range(2):
            unit = unit_facts(facts, w, dx)
            for dy in range(2):
                out[dx, dy] = fetch(unit, dy, own, other, unit[2] * rows, rows)


def load_queries(unit, own, other, q_all):
    rows = q_all.shape[0] // (2 * GROUP)
    for dy in range(2):
        for g in range(GROUP):
            row = (unit[2] * GROUP + g) * rows
            at = (g * 2 + dy) * rows
            q_all[at : at + rows, :] = fetch(unit, dy, own, other, row, rows)


def online_step(q, k, v, mask, state):
    top, total, mixed = state
    scores = lax.dot_general(k, q, (((1,), (1,)), ((), ())), preferred_element_type=jnp.float32)
    scores = scores * SCORE_FACTOR
    if mask is not None:
        scores = jnp.where(mask, scores, LOWEST)
    new_top = jnp.maximum(top, jnp.max(scores, axis=0, keepdims=True))
    scale = jnp.exp2(top - new_top)
    weights = jnp.exp2(scores - new_top)
    total = total * scale + jnp.sum(weights, axis=0, keepdims=True)
    mixed = mixed * scale + lax.dot_general(
        v, weights.astype(jnp.bfloat16), (((0,), (0,)), ((), ())),
        preferred_element_type=jnp.float32,
    )
    return new_top, total, mixed


def device_place():
    group, seq = lax.axis_index("cand"), lax.axis_index("seq")
    return group // 2, group % 2, seq // 2, seq % 2


def prompt_kernel(layout, w, chunk, facts, own, other, *refs):
    q_out, mixed_ref, top_ref, total_ref, k_all, v_all = refs
    x, core, r, y = device_place()
    rows = k_all.shape[0] // (8 * layout.rings)
    queries = q_out.shape[1]
    first = own.shape[1] - 2 * layout.rings * rows
    for o, piece in enumerate((own, other)):
        for k in range(layout.rings):
            for d in range(4):
                group = (x ^ (d >> 1)) * 2 + (core ^ o)
                seq = lax.rem(r + layout.rings - k, layout.rings) * 2 + (y ^ (d & 1))
                at = pl.multiple_of((group * layout.rings * 2 + seq) * rows, rows)
                for half, target in enumerate((k_all, v_all)):
                    here = first + (half * layout.rings + k) * rows
                    target[pl.ds(at, rows), :] = piece[d, here : here + rows, :]
    for n in range(2):
        unit = unit_facts(facts, w, n)
        length, offset = unit[3], unit[4]

        @pl.when(r * (queries // GROUP) < length)
        def _():
            q_all = q_out.at[n]
            load_queries(unit, own, other, q_all)

            def run(at, size, state, masked):
                mask = None
                if masked:
                    place = lax.broadcasted_iota(jnp.int32, (size, queries), 0) + at
                    mask = place < offset
                return online_step(
                    q_all[...], k_all[pl.ds(at, size), :], v_all[pl.ds(at, size), :], mask, state
                )

            def whole(i, state):
                return run(pl.multiple_of(i * chunk, chunk), chunk, state, False)

            def part(i, state):
                return run(pl.multiple_of(i * (chunk // 2), chunk // 2), chunk // 2, state, True)

            state = (
                jnp.full((1, queries), LOWEST, jnp.float32),
                jnp.zeros((1, queries), jnp.float32),
                jnp.zeros((HEAD, queries), jnp.float32),
            )
            count = offset // chunk
            state = lax.fori_loop(0, count, whole, state)
            end = (offset + chunk // 2 - 1) // (chunk // 2)
            state = lax.fori_loop(count * 2, end, part, state)
            top_ref[n], total_ref[n], mixed_ref[n] = state


def query_places(first, swap, rows, queries):
    column = lax.broadcasted_iota(jnp.int32, (1, queries), 1)
    for g in range(GROUP - 1, 0, -1):
        column = jnp.where(column >= g * 2 * rows, column - g * 2 * rows, column)
    second = column >= rows
    row = jnp.where(second, column - rows, column)
    upper = jnp.where(second, 1 - swap, swap)
    return first + upper * rows + row


def response_kernel(layout, w, dx, facts, q_all, mixed, top, total, *refs):
    pieces = refs[: layout.rings]
    outs = refs[layout.rings : 2 + layout.rings]
    k_all, v_all = refs[2 + layout.rings :]
    _, _, r, y = device_place()
    rows = outs[0].shape[0]
    queries = q_all.shape[1]
    unit = unit_facts(facts, w, dx)
    length = unit[3]

    @pl.when(r * (2 * rows) >= length)
    def _():
        for out in outs:
            out[...] = jnp.zeros(out.shape, out.dtype)

    @pl.when(r * (2 * rows) < length)
    def _():
        for k, piece in enumerate(pieces):

            @pl.when(k <= r)
            def _():
                for dy in range(2):
                    at = pl.multiple_of(((r - k) * 2 + (y ^ dy)) * rows, rows)
                    k_all[pl.ds(at, rows), :] = piece[dx, dy, :, :HEAD]
                    v_all[pl.ds(at, rows), :] = piece[dx, dy, :, HEAD:]

        place = query_places(r * (2 * rows), y, rows, queries)
        top_ref, total_ref, mixed_ref = top.at[dx], total.at[dx], mixed.at[dx]
        half = 2 * rows

        def run(at, size, state):
            at = pl.multiple_of(at, half)
            key = lax.broadcasted_iota(jnp.int32, (size, queries), 0) + at
            mask = key <= jnp.minimum(place, length - 1)
            return online_step(
                q_all[dx], k_all[pl.ds(at, size), :], v_all[pl.ds(at, size), :], mask, state
            )

        last = jnp.minimum((r + 1) * half, length)
        count = (last + half - 1) // (2 * half)
        state = (top_ref[...], total_ref[...], mixed_ref[...])
        state = lax.fori_loop(
            0, count, lambda i, s: run(i * (2 * half), 2 * half, s), state
        )
        rest = (last - count * (2 * half) + half - 1) // half
        _, sums, result = lax.fori_loop(
            0, rest, lambda i, s: run(count * (2 * half), half, s), state
        )
        result = jnp.where(place < length, result * (1.0 / sums), 0.0).astype(jnp.bfloat16).T
        for dy, out in enumerate(outs):
            for g in range(GROUP):
                at = (g * 2 + dy) * rows
                out[:, g * HEAD : (g + 1) * HEAD] = result[at : at + rows]


def join_kernel(*refs):
    pieces, out = refs[:-1], refs[-1]
    own = own_head()
    for w in range(out.shape[0]):
        for d in range(4):
            lane = pl.ds(pl.multiple_of((own ^ d) * WIDE, HEAD), WIDE)
            out[w, :, lane] = pieces[w * 4 + d][...]


def divisor(total, *choices):
    for choice in choices:
        if total % choice == 0:
            return choice
    return total


def struct(*shape, dtype=jnp.bfloat16):
    return jax.ShapeDtypeStruct(shape, dtype)


def after(value, *others):
    return lax.optimization_barrier((value, *others))[0]


def body(layout, q, rk, rv, pk, pv, lengths, offsets, ranks):
    cands, rows = q.shape[0], q.shape[1]
    queries = 2 * rows * GROUP
    bf16 = functools.partial(pltpu.VMEM, dtype=jnp.bfloat16)

    def exchange(pieces, *held):
        got = layout.exchange(pieces)
        if held:
            got[0] = after(got[0], *held)
        own = kernel_call(
            stack_kernel, struct(4, *got[0].shape), got, name="stack", scalars=0
        )
        return own, layout.permute(own, core=1)

    facts = jnp.concatenate([lengths, offsets, ranks])
    anywhere = pl.BlockSpec(memory_space=pl.ANY)
    *keys, prompt = pl.pallas_call(
        pack_first_kernel,
        out_shape=[struct(cands * rows, 2 * HEAD)] * 4 + [struct(pk.shape[0], 2 * pk.shape[1])],
        in_specs=[anywhere] * 4,
        out_specs=[VMEM] * 5,
        scratch_shapes=[pltpu.SemaphoreType.DMA((2 + 8 * cands,))],
        compiler_params=pltpu.CompilerParams(vmem_limit_bytes=PACK_VMEM),
        name="pack_first",
    )(rk, rv, pk, pv)
    prompt = layout.spread(prompt)
    asked = kernel_call(
        pack_queries_kernel,
        [struct(cands * GROUP * rows, HEAD)] * 4,
        (q,),
        name="pack_queries",
        scalars=0,
    )
    keys[3] = after(keys[3], asked[0])
    prompt_rows = layout.rings * pk.shape[0]
    packed = kernel_call(
        functools.partial(pack_kernel, layout.rings),
        [struct(cands * GROUP * rows + 2 * prompt_rows, HEAD)] * 4,
        (*asked, pk, pv, *prompt[1:]),
        name="pack_queries_prompt",
        scalars=0,
    )
    keys, keys_other = exchange(keys, packed[0])
    slots = kernel_call(
        select_keys_kernel,
        [struct(2, 2, rows, 2 * HEAD)] * cands,
        (facts, keys, keys_other),
        name="select_keys",
    )
    pieces = [layout.spread(slots[0])]
    for w in range(1, cands):
        pieces.append(layout.spread(after(slots[w], pieces[0][1])))
    packed = exchange(packed, pieces[0][1], pieces[0][2])

    prompt_keys = 8 * prompt_rows
    response_keys = layout.rings * 2 * rows
    chunk = divisor(prompt_keys, 1024, 512, 256)
    states = []
    for w in range(cands):
        states.append(
            kernel_call(
                functools.partial(prompt_kernel, layout, w, chunk),
                [
                    struct(2, queries, HEAD),
                    struct(2, HEAD, queries, dtype=jnp.float32),
                    struct(2, 1, queries, dtype=jnp.float32),
                    struct(2, 1, queries, dtype=jnp.float32),
                ],
                (facts, *packed),
                scratch=[bf16((prompt_keys, HEAD))] * 2,
                cost=(8 * queries * prompt_keys * HEAD, 4 * prompt_keys * HEAD),
                name="prompt_part",
                spare=16 << 20,
            )
        )
    finished = []
    for w in range(cands):
        outs = [None] * 4
        for dx in (1, 0):
            outs[dx * 2], outs[dx * 2 + 1] = kernel_call(
                functools.partial(response_kernel, layout, w, dx),
                [struct(rows, WIDE)] * 2,
                (facts, *states[w], *pieces[w]),
                scratch=[bf16((response_keys, HEAD))] * 2,
                cost=(4 * queries * response_keys * HEAD, 2 * response_keys * HEAD),
                name="response_part",
                spare=12 << 20,
            )
        finished += layout.exchange(outs)
    return kernel_call(join_kernel, struct(*q.shape), finished, name="join_heads", scalars=0)


def solution(mesh):
    in_specs = (
        P("cand", "seq", None),
        P("cand", "seq", None),
        P("cand", "seq", None),
        P(("cand", "seq"), None),
        P(("cand", "seq"), None),
        P(),
        P(),
        P(),
    )
    return jax.shard_map(
        functools.partial(body, Layout(mesh)),
        mesh=mesh,
        in_specs=in_specs,
        out_specs=P("cand", "seq", None),
        check_vma=False,
    )
```

```python
import functools
import math

import jax
import jax.numpy as jnp
from jax import lax
from jax.experimental import pallas as pl
from jax.experimental.pallas import tpu as pltpu
from jax.sharding import PartitionSpec as P

QUERY_HEADS = 20
KEY_VALUE_HEADS = 4
HEAD = 128
GROUP = QUERY_HEADS // KEY_VALUE_HEADS
WIDE = GROUP * HEAD
SCORE_FACTOR = math.log2(math.e) / math.sqrt(HEAD)
LOWEST = -1e30
AXES = ("cand", "seq")
PACK_VMEM = 60 << 20
VMEM = pl.BlockSpec(memory_space=pltpu.VMEM)
SMEM = pl.BlockSpec(memory_space=pltpu.SMEM)


class Layout:
    def __init__(self, mesh):
        assert mesh.shape["cand"] == 4 and mesh.shape["seq"] % 2 == 0
        self.rings = mesh.shape["seq"] // 2

    def permute(self, array, d=0, core=0, ring=0):
        pairs = []
        for x in range(2):
            for c in range(2):
                for r in range(self.rings):
                    for y in range(2):
                        source = ((x * 2 + c) * self.rings + r) * 2 + y
                        target = ((x ^ (d >> 1)) * 2 + (c ^ core)) * self.rings
                        target = (target + (r + ring) % self.rings) * 2 + (y ^ (d & 1))
                        pairs.append((source, target))
        return lax.ppermute(array, AXES, pairs)

    def exchange(self, pieces):
        return [pieces[0]] + [self.permute(pieces[d], d=d) for d in range(1, 4)]

    def spread(self, block):
        return [block] + [self.permute(block, ring=k) for k in range(1, self.rings)]

    def ring_gather(self, block):
        pieces = [block]
        for _ in range(self.rings - 1):
            pieces.append(self.permute(pieces[-1], ring=1))
        return pieces


def kernel_call(kernel, out_shape, operands, scratch=(), cost=(0, 0), name=None, scalars=1, spare=2 << 20):
    many = isinstance(out_shape, list)
    arrays = list(operands) + (list(out_shape) if many else [out_shape]) + list(scratch)
    held = sum(math.prod(a.shape) * jnp.dtype(a.dtype).itemsize for a in arrays)
    return pl.pallas_call(
        kernel,
        out_shape=out_shape,
        in_specs=[SMEM] * scalars + [VMEM] * (len(operands) - scalars),
        out_specs=[VMEM] * len(out_shape) if many else VMEM,
        scratch_shapes=list(scratch),
        compiler_params=pltpu.CompilerParams(vmem_limit_bytes=held + held // 4 + spare),
        cost_estimate=pl.CostEstimate(
            flops=cost[0], transcendentals=cost[0] // 512, bytes_accessed=cost[1]
        ),
        name=name,
    )(*operands)


def own_head():
    return lax.axis_index("cand") // 2 * 2 + lax.axis_index("seq") % 2


def pack_first_kernel(rk, rv, pk, pv, *refs):
    outs, joined, sems = refs[:4], refs[4], refs[5]
    own = own_head()
    cands, rows = rk.shape[0], rk.shape[1]
    moves = []
    width = pk.shape[1]
    for half, source in enumerate((pk, pv)):
        moves.append((source, joined.at[:, pl.ds(half * width, width)]))
    for d, out in enumerate(outs):
        lane = pl.ds(pl.multiple_of((own ^ d) * HEAD, HEAD), HEAD)
        for half, source in enumerate((rk, rv)):
            for w in range(cands):
                target = out.at[pl.ds(w * rows, rows), pl.ds(half * HEAD, HEAD)]
                moves.append((source.at[w, :, lane], target))
    copies = [pltpu.make_async_copy(a, b, sems.at[n]) for n, (a, b) in enumerate(moves)]
    for copy in copies:
        copy.start()
    for copy in copies:
        copy.wait()


def pack_queries_kernel(q, *outs):
    own = own_head()
    cands, rows = q.shape[0], q.shape[1]
    for d, out in enumerate(outs):
        for w in range(cands):
            for g in range(GROUP):
                lane = pl.multiple_of((own ^ d) * WIDE + g * HEAD, HEAD)
                at = (w * GROUP + g) * rows
                out[at : at + rows, :] = q[w, :, pl.ds(lane, HEAD)]


def pack_kernel(rings, *refs):
    asked, mine, pieces, outs = refs[:4], refs[4:6], refs[6 : 5 + rings], refs[5 + rings :]
    own = own_head()
    rows, width = pieces[0].shape
    for d, out in enumerate(outs):
        first = asked[d].shape[0]
        out[:first, :] = asked[d][...]
        for half in range(2):
            lane = pl.multiple_of((own ^ d) * HEAD + half * (width // 2), HEAD)
            at = first + half * rings * rows
            mine_lane = pl.ds(pl.multiple_of((own ^ d) * HEAD, HEAD), HEAD)
            out[at : at + rows, :] = mine[half][:, mine_lane]
            for k, piece in enumerate(pieces):
                at = first + (half * rings + k + 1) * rows
                out[at : at + rows, :] = piece[:, pl.ds(lane, HEAD)]


def stack_kernel(*refs):
    for n, piece in enumerate(refs[:-1]):
        refs[-1][n] = piece[...]


def unit_facts(facts, w, dx):
    group, count = lax.axis_index("cand"), facts.shape[0] // 3
    x, core = group // 2, group % 2
    cands = count // 4
    rank = ((x ^ dx) * 2 + core) * cands + w
    source = jnp.int32(0)
    for c in range(count):
        source = jnp.where(facts[2 * count + c] == rank, c, source)
    home = source // cands
    away = (home % 2) ^ core
    return away, (home // 2) ^ x, source % cands, facts[source], facts[count + source]


def fetch(unit, dy, own, other, row, rows):
    d = unit[1] * 2 + dy
    at = pl.ds(pl.multiple_of(row, rows), rows)
    return jnp.where(unit[0] == 1, other[d, at, :], own[d, at, :])


def select_keys_kernel(facts, own, other, *outs):
    rows = outs[0].shape[2]
    for w, out in enumerate(outs):
        for dx in range(2):
            unit = unit_facts(facts, w, dx)
            for dy in range(2):
                out[dx, dy] = fetch(unit, dy, own, other, unit[2] * rows, rows)


def load_queries(unit, own, other, q_all):
    rows = q_all.shape[0] // (2 * GROUP)
    for dy in range(2):
        for g in range(GROUP):
            row = (unit[2] * GROUP + g) * rows
            at = (g * 2 + dy) * rows
            q_all[at : at + rows, :] = fetch(unit, dy, own, other, row, rows)


def online_step(q, k, v, mask, state):
    top, total, mixed = state
    scores = lax.dot_general(k, q, (((1,), (1,)), ((), ())), preferred_element_type=jnp.float32)
    scores = scores * SCORE_FACTOR
    if mask is not None:
        scores = jnp.where(mask, scores, LOWEST)
    new_top = jnp.maximum(top, jnp.max(scores, axis=0, keepdims=True))
    scale = jnp.exp2(top - new_top)
    weights = jnp.exp2(scores - new_top)
    total = total * scale + jnp.sum(weights, axis=0, keepdims=True)
    mixed = mixed * scale + lax.dot_general(
        v, weights.astype(jnp.bfloat16), (((0,), (0,)), ((), ())),
        preferred_element_type=jnp.float32,
    )
    return new_top, total, mixed


def device_place():
    group, seq = lax.axis_index("cand"), lax.axis_index("seq")
    return group // 2, group % 2, seq // 2, seq % 2


def prompt_kernel(layout, w, chunk, facts, own, other, *refs):
    q_out, mixed_ref, top_ref, total_ref, k_all, v_all = refs
    x, core, r, y = device_place()
    rows = k_all.shape[0] // (8 * layout.rings)
    queries = q_out.shape[1]
    first = own.shape[1] - 2 * layout.rings * rows
    for o, piece in enumerate((own, other)):
        for k in range(layout.rings):
            for d in range(4):
                group = (x ^ (d >> 1)) * 2 + (core ^ o)
                seq = lax.rem(r + layout.rings - k, layout.rings) * 2 + (y ^ (d & 1))
                at = pl.multiple_of((group * layout.rings * 2 + seq) * rows, rows)
                for half, target in enumerate((k_all, v_all)):
                    here = first + (half * layout.rings + k) * rows
                    target[pl.ds(at, rows), :] = piece[d, here : here + rows, :]
    for n in range(2):
        unit = unit_facts(facts, w, n)
        length, offset = unit[3], unit[4]

        @pl.when(r * (queries // GROUP) < length)
        def _():
            q_all = q_out.at[n]
            load_queries(unit, own, other, q_all)

            def run(at, size, state, masked):
                mask = None
                if masked:
                    place = lax.broadcasted_iota(jnp.int32, (size, queries), 0) + at
                    mask = place < offset
                return online_step(
                    q_all[...], k_all[pl.ds(at, size), :], v_all[pl.ds(at, size), :], mask, state
                )

            def whole(i, state):
                return run(pl.multiple_of(i * chunk, chunk), chunk, state, False)

            def most(i, state):
                return run(pl.multiple_of(i * chunk, chunk), chunk, state, True)

            def part(i, state):
                return run(pl.multiple_of(i * chunk, chunk), chunk // 2, state, True)

            state = (
                jnp.full((1, queries), LOWEST, jnp.float32),
                jnp.zeros((1, queries), jnp.float32),
                jnp.zeros((HEAD, queries), jnp.float32),
            )
            count = offset // chunk
            state = lax.fori_loop(0, count, whole, state)
            rest = offset - count * chunk
            halves = (rest + chunk // 2 - 1) // (chunk // 2)
            state = lax.fori_loop(count, count + halves // 2, most, state)
            state = lax.fori_loop(count, count + halves % 2, part, state)
            top_ref[n], total_ref[n], mixed_ref[n] = state


def query_places(first, swap, rows, queries):
    column = lax.broadcasted_iota(jnp.int32, (1, queries), 1)
    for g in range(GROUP - 1, 0, -1):
        column = jnp.where(column >= g * 2 * rows, column - g * 2 * rows, column)
    second = column >= rows
    row = jnp.where(second, column - rows, column)
    upper = jnp.where(second, 1 - swap, swap)
    return first + upper * rows + row


def response_kernel(layout, w, dx, facts, q_all, mixed, top, total, *refs):
    pieces = refs[: layout.rings]
    outs = refs[layout.rings : 2 + layout.rings]
    k_all, v_all = refs[2 + layout.rings :]
    _, _, r, y = device_place()
    rows = outs[0].shape[0]
    queries = q_all.shape[1]
    unit = unit_facts(facts, w, dx)
    length = unit[3]

    @pl.when(r * (2 * rows) >= length)
    def _():
        for out in outs:
            out[...] = jnp.zeros(out.shape, out.dtype)

    @pl.when(r * (2 * rows) < length)
    def _():
        for k, piece in enumerate(pieces):

            @pl.when(k <= r)
            def _():
                for dy in range(2):
                    at = pl.multiple_of(((r - k) * 2 + (y ^ dy)) * rows, rows)
                    k_all[pl.ds(at, rows), :] = piece[dx, dy, :, :HEAD]
                    v_all[pl.ds(at, rows), :] = piece[dx, dy, :, HEAD:]

        place = query_places(r * (2 * rows), y, rows, queries)
        top_ref, total_ref, mixed_ref = top.at[dx], total.at[dx], mixed.at[dx]
        half = 2 * rows

        def run(at, size, state):
            at = pl.multiple_of(at, half)
            key = lax.broadcasted_iota(jnp.int32, (size, queries), 0) + at
            mask = key <= jnp.minimum(place, length - 1)
            return online_step(
                q_all[dx], k_all[pl.ds(at, size), :], v_all[pl.ds(at, size), :], mask, state
            )

        last = jnp.minimum((r + 1) * half, length)
        count = (last + half - 1) // (2 * half)
        state = (top_ref[...], total_ref[...], mixed_ref[...])
        state = lax.fori_loop(
            0, count, lambda i, s: run(i * (2 * half), 2 * half, s), state
        )
        rest = (last - count * (2 * half) + half - 1) // half
        _, sums, result = lax.fori_loop(
            0, rest, lambda i, s: run(count * (2 * half), half, s), state
        )
        result = jnp.where(place < length, result * (1.0 / sums), 0.0).astype(jnp.bfloat16).T
        for dy, out in enumerate(outs):
            for g in range(GROUP):
                at = (g * 2 + dy) * rows
                out[:, g * HEAD : (g + 1) * HEAD] = result[at : at + rows]


def join_kernel(*refs):
    pieces, out = refs[:-1], refs[-1]
    own = own_head()
    for w in range(out.shape[0]):
        for d in range(4):
            lane = pl.ds(pl.multiple_of((own ^ d) * WIDE, HEAD), WIDE)
            out[w, :, lane] = pieces[w * 4 + d][...]


def divisor(total, *choices):
    for choice in choices:
        if total % choice == 0:
            return choice
    return total


def struct(*shape, dtype=jnp.bfloat16):
    return jax.ShapeDtypeStruct(shape, dtype)


def after(value, *others):
    return lax.optimization_barrier((value, *others))[0]


def body(layout, q, rk, rv, pk, pv, lengths, offsets, ranks):
    cands, rows = q.shape[0], q.shape[1]
    queries = 2 * rows * GROUP
    bf16 = functools.partial(pltpu.VMEM, dtype=jnp.bfloat16)

    def exchange(pieces, *held):
        got = layout.exchange(pieces)
        if held:
            got[0] = after(got[0], *held)
        own = kernel_call(
            stack_kernel, struct(4, *got[0].shape), got, name="stack", scalars=0
        )
        return own, layout.permute(own, core=1)

    facts = jnp.concatenate([lengths, offsets, ranks])
    anywhere = pl.BlockSpec(memory_space=pl.ANY)
    *keys, prompt = pl.pallas_call(
        pack_first_kernel,
        out_shape=[struct(cands * rows, 2 * HEAD)] * 4 + [struct(pk.shape[0], 2 * pk.shape[1])],
        in_specs=[anywhere] * 4,
        out_specs=[VMEM] * 5,
        scratch_shapes=[pltpu.SemaphoreType.DMA((2 + 8 * cands,))],
        compiler_params=pltpu.CompilerParams(vmem_limit_bytes=PACK_VMEM),
        name="pack_first",
    )(rk, rv, pk, pv)
    prompt = layout.spread(prompt)
    asked = kernel_call(
        pack_queries_kernel,
        [struct(cands * GROUP * rows, HEAD)] * 4,
        (q,),
        name="pack_queries",
        scalars=0,
    )
    keys[3] = after(keys[3], asked[0])
    prompt_rows = layout.rings * pk.shape[0]
    packed = kernel_call(
        functools.partial(pack_kernel, layout.rings),
        [struct(cands * GROUP * rows + 2 * prompt_rows, HEAD)] * 4,
        (*asked, pk, pv, *prompt[1:]),
        name="pack_queries_prompt",
        scalars=0,
    )
    keys, keys_other = exchange(keys, packed[0])
    slots = kernel_call(
        select_keys_kernel,
        [struct(2, 2, rows, 2 * HEAD)] * cands,
        (facts, keys, keys_other),
        name="select_keys",
    )
    pieces = [layout.spread(slots[0])]
    packed = exchange(packed, pieces[0][1], pieces[0][2])
    for w in range(1, cands):
        pieces.append(layout.spread(after(slots[w], packed[0])))

    prompt_keys = 8 * prompt_rows
    response_keys = layout.rings * 2 * rows
    chunk = divisor(prompt_keys, 1024, 512, 256)
    states = []
    for w in range(cands):
        states.append(
            kernel_call(
                functools.partial(prompt_kernel, layout, w, chunk),
                [
                    struct(2, queries, HEAD),
                    struct(2, HEAD, queries, dtype=jnp.float32),
                    struct(2, 1, queries, dtype=jnp.float32),
                    struct(2, 1, queries, dtype=jnp.float32),
                ],
                (facts, *packed),
                scratch=[bf16((prompt_keys, HEAD))] * 2,
                cost=(8 * queries * prompt_keys * HEAD, 4 * prompt_keys * HEAD),
                name="prompt_part",
                spare=16 << 20,
            )
        )
    finished = []
    for w in range(cands):
        outs = [None] * 4
        for dx in (1, 0):
            outs[dx * 2], outs[dx * 2 + 1] = kernel_call(
                functools.partial(response_kernel, layout, w, dx),
                [struct(rows, WIDE)] * 2,
                (facts, *states[w], *pieces[w]),
                scratch=[bf16((response_keys, HEAD))] * 2,
                cost=(4 * queries * response_keys * HEAD, 2 * response_keys * HEAD),
                name="response_part",
                spare=12 << 20,
            )
        finished += layout.exchange(outs)
    return kernel_call(join_kernel, struct(*q.shape), finished, name="join_heads", scalars=0)


def solution(mesh):
    in_specs = (
        P("cand", "seq", None),
        P("cand", "seq", None),
        P("cand", "seq", None),
        P(("cand", "seq"), None),
        P(("cand", "seq"), None),
        P(),
        P(),
        P(),
    )
    return jax.shard_map(
        functools.partial(body, Layout(mesh)),
        mesh=mesh,
        in_specs=in_specs,
        out_specs=P("cand", "seq", None),
        check_vma=False,
    )
```
